32 devices in a mesh: node: 4 (over y, x), local: 4 (over z), rep: 2 (over core).
Axes of the slice: x: 2, y: 2, z: 4, core: 2. Of those that a mesh axis runs over, the one named last changes fastest.
Arguments:
- grad_out: bfloat16 [256, 4096], P(('node', 'local', 'rep')), may hold values from -0.59765625 to 0.59765625
- expert_ids: int32 [256, 4], P(('node', 'local', 'rep')), may hold values from 0 to 15, as said below
- route_weights: bfloat16 [256, 4], P(('node', 'local', 'rep')), may hold values from 0.19921875 to 2
- gate_pre: bfloat16 [128, 16384], P('rep', ('node', 'local')), may hold values from -6 to 6
- up_pre: bfloat16 [128, 16384], P('rep', ('node', 'local')), may hold values from -6 to 6
- w_down_t: bfloat16 [4096, 16384], P(None, ('node', 'local')), may hold values from -0.1875 to 0.1875
Outputs:
- grad_gate_pre: bfloat16 [128, 16384], P('rep', ('node', 'local'))
- grad_up_pre: bfloat16 [128, 16384], P('rep', ('node', 'local'))
- grad_down_t: bfloat16 [4096, 16384], P('rep', ('node', 'local'))
- grad_route: bfloat16 [256, 16], P(('local', 'rep'), 'node')
The draws below stay inside these ranges and needn't reach their ends.
Inputs may be any that keep to these rules, and one draw needn't show every extreme that they name: `expert_ids`: each token names 4 different experts: 2 in each of 2 different groups (group of e = e // 4). In every cohort each group is named by exactly 16 tokens, and within it exactly 1 expert are named 16 times, 2 experts 8 times and the others never. In every group one expert is named 16 times by every cohort.
All inputs are finite; a program needn't handle non-finite values.
Results may differ from the reference program's by a relative error of at most 0.013.
Values may be sent and summed in bfloat16 or wider, within the bound.
A program may use at most 64 MiB of HBM per device.

```python
import math
from functools import partial
import jax
import jax.numpy as jnp
from jax import lax

D = 4096
H = 1024
PER_GROUP = 2
TOK_DEV = 8
GROUPS_TOK = 2
TOP = 4
OWNERS = 1
HS = 1024
EXP_GROUP = 4
EXPERTS = 16
TOKENS = 256
COHORT = 32
HALF = 8
CAP = 16
FULL = 1
SLOTS = 64
N_NODE = 4
N_LOCAL = 4
N_REP = 2


def group_ranking(group_key, hot_expert):
    scores_int = jax.random.permutation(group_key, EXP_GROUP).astype(jnp.int32)
    scores_int = jnp.where(jnp.arange(EXP_GROUP, dtype=jnp.int32) == hot_expert, -1, scores_int)
    return jnp.argsort(scores_int, stable=True).astype(jnp.int32)


def cohort_routes(hot_experts, cohort_key):
    key_list = jax.random.split(cohort_key, 3)
    group_order = jax.random.permutation(key_list[0], N_NODE).astype(jnp.int32)
    token_order = jax.random.permutation(key_list[1], COHORT).astype(jnp.int32)
    expert_keys = jax.random.split(key_list[2], N_NODE)
    ranking = jax.vmap(group_ranking)(expert_keys, hot_experts)
    position = jnp.arange(COHORT, dtype=jnp.int32)
    choice_col = jnp.arange(GROUPS_TOK, dtype=jnp.int32)
    group_rank = (GROUPS_TOK * position[:, None] + choice_col[None, :]) % N_NODE
    chooses = jnp.sum((group_rank[:, :, None] == jnp.arange(N_NODE, dtype=jnp.int32)[None, None, :]).astype(jnp.int32), axis=1)
    before = jnp.cumsum(chooses, axis=0) - chooses
    token_rank = jnp.take_along_axis(before, group_rank, axis=1)
    pick_col = jnp.arange(PER_GROUP, dtype=jnp.int32)
    pick_index = token_rank[:, :, None] + TOK_DEV * GROUPS_TOK * pick_col[None, None, :]
    expert_rank = jnp.where(pick_index < FULL * CAP, pick_index // CAP, FULL + (pick_index - FULL * CAP) // HALF)
    group_id = group_order[group_rank]
    chosen = ranking[group_id[:, :, None], expert_rank]
    expert_id = group_id[:, :, None] * EXP_GROUP + chosen
    virtual = expert_id.reshape(COHORT, TOP)
    return virtual[jnp.argsort(token_order, stable=True)]


def draw_expert_ids(key, part):
    key_pair = jax.random.split(jax.random.fold_in(key, 11))
    hot_experts = jax.random.randint(key_pair[0], (N_NODE,), 0, EXP_GROUP).astype(jnp.int32)
    cohort_keys = jax.random.split(key_pair[1], N_LOCAL * N_REP)
    routes = jax.vmap(partial(cohort_routes, hot_experts))(cohort_keys)
    routes = routes.reshape(N_LOCAL, N_REP, N_NODE, TOK_DEV, TOP).transpose(2, 0, 1, 3, 4)
    return routes.reshape(TOKENS, TOP).astype(jnp.int32)


def steps_of(own_key, dims, shards, smallest, largest):
    factor_of, own = 1.0, jax.random.fold_in(own_key, 6)
    for dim, shards_of in shards:
        draws = jnp.exp(jax.random.uniform(jax.random.fold_in(own, dim), (shards_of,), jnp.float32, smallest / len(shards), largest / len(shards)))
        factor_of = factor_of * jnp.repeat(draws, dims[dim] // shards_of).reshape([-1 if axis == dim else 1 for axis in range(len(dims))])
    return factor_of


def scatter_about(key, dims, spread, reach, pieces=(), kind=jnp.bfloat16):
    values = jax.random.normal(key, dims, jnp.float32) * spread
    if len(pieces) > 0:
        values = steps_of(key, dims, pieces, -0.22, 0.18) * values
    return jnp.clip(values, min=-reach, max=reach).astype(kind)


def setup_inputs(seed: int = 0) -> dict:
    key_of = jax.random.split(jax.random.key(seed), 7)
    grad_out = scatter_about(key_of[0], (TOKENS, D), 0.1, 0.59765625, ((0, 32),))
    expert_ids = draw_expert_ids(jax.random.fold_in(key_of[6], 71), 0)
    route_weights = jnp.clip(jnp.exp(math.log(2.0) - 2.306499 * jax.random.uniform(key_of[2], (TOKENS, TOP), jnp.float32) ** steps_of(key_of[2], (TOKENS, TOP), ((0, 32),), -0.2, 0.2)), 0.19921875, 2.0).astype(jnp.bfloat16)
    gate_pre = scatter_about(key_of[3], (N_REP * SLOTS, EXPERTS * H), 1.0, 6.0, ((0, 2), (1, 16)))
    up_pre = scatter_about(key_of[4], (N_REP * SLOTS, EXPERTS * H), 1.0, 6.0, ((0, 2), (1, 16)))
    w_down_t = scatter_about(key_of[5], (D, EXPERTS * H), H ** -0.5, 0.1875, ((1, 16),))
    return dict(grad_out=grad_out, expert_ids=expert_ids, route_weights=route_weights, gate_pre=gate_pre, up_pre=up_pre, w_down_t=w_down_t)


def to_cohorts(array):
    tail = array.shape[1]
    shaped = array.reshape(N_NODE, N_LOCAL, N_REP, TOK_DEV, tail)
    return shaped.transpose(1, 2, 0, 3, 4).reshape(N_LOCAL, N_REP, COHORT, tail)


def reference(grad_out, expert_ids, route_weights, gate_pre, up_pre, w_down_t):
    ids_cohort = to_cohorts(expert_ids)
    weights_cohort = to_cohorts(route_weights)
    grad_cohort = to_cohorts(grad_out)
    expert_range = jnp.arange(EXPERTS, dtype=jnp.int32)
    route_hits = (ids_cohort[..., None] == expert_range).astype(jnp.int32)
    per_expert = jnp.sum(route_hits, axis=3)
    earlier = jnp.cumsum(per_expert, axis=2) - per_expert
    slot_index = jnp.sum(route_hits * earlier[:, :, :, None, :], axis=4).astype(jnp.int32)
    local_index = jnp.arange(N_LOCAL, dtype=jnp.int32)[:, None, None, None]
    replica_index = jnp.arange(N_REP, dtype=jnp.int32)[None, :, None, None]
    flat_index = (((ids_cohort * N_REP + replica_index) * N_LOCAL + local_index) * CAP + slot_index).astype(jnp.int32)
    flat_index = flat_index.reshape(-1)
    total_rows = EXPERTS * N_REP * SLOTS
    source_rows = jnp.broadcast_to(grad_cohort[:, :, :, None, :], (N_LOCAL, N_REP, COHORT, TOP, D)).reshape(-1, D)
    packed = jnp.zeros((total_rows, D), jnp.bfloat16).at[flat_index].set(source_rows)
    packed = packed.reshape(EXPERTS, N_REP * SLOTS, D)
    packed_weights = jnp.zeros((total_rows,), jnp.float32).at[flat_index].set(weights_cohort.reshape(-1).astype(jnp.float32))
    packed_weights = packed_weights.reshape(EXPERTS, N_REP * SLOTS)

    def one_expert(expert_index):
        cotangent = lax.dynamic_index_in_dim(packed, expert_index, 0, keepdims=False)
        weight = lax.dynamic_index_in_dim(packed_weights, expert_index, 0, keepdims=False)[:, None]
        column_start = expert_index * H
        gate_value = lax.dynamic_slice_in_dim(gate_pre, column_start, H, 1).astype(jnp.float32)
        up_value = lax.dynamic_slice_in_dim(up_pre, column_start, H, 1).astype(jnp.float32)
        down_cols = lax.dynamic_slice_in_dim(w_down_t, column_start, H, 1)
        backward = jnp.dot(cotangent, down_cols, preferred_element_type=jnp.float32)
        sigmoid_gate = jax.nn.sigmoid(gate_value)
        activated = gate_value * sigmoid_gate
        hidden = activated * up_value
        shares = jnp.sum((hidden * backward).reshape(N_REP * SLOTS, OWNERS, HS), axis=2).astype(jnp.bfloat16)
        score_value = jnp.sum(shares.astype(jnp.float32), axis=1).astype(jnp.bfloat16)
        scaled = weight * backward
        grad_gate = (scaled * up_value * sigmoid_gate * (1.0 + gate_value * (1.0 - sigmoid_gate))).astype(jnp.bfloat16)
        grad_up = (scaled * activated).astype(jnp.bfloat16)
        weighted = (weight * hidden).astype(jnp.bfloat16)
        total = jnp.zeros((D, H), jnp.float32)
        for replica in range(N_REP):
            term = lax.dot_general(cotangent[replica * SLOTS:(replica + 1) * SLOTS], weighted[replica * SLOTS:(replica + 1) * SLOTS], (((0,), (0,)), ((), ())), preferred_element_type=jnp.float32)
            total = total + term.astype(jnp.bfloat16).astype(jnp.float32)
        return score_value, grad_gate, grad_up, total.astype(jnp.bfloat16)

    score_all, gate_all, up_all, down_all = lax.map(one_expert, jnp.arange(EXPERTS, dtype=jnp.int32))
    grad_gate_pre = gate_all.transpose(1, 0, 2).reshape(N_REP * SLOTS, EXPERTS * H)
    grad_up_pre = up_all.transpose(1, 0, 2).reshape(N_REP * SLOTS, EXPERTS * H)
    grad_down_t = down_all.transpose(1, 0, 2).reshape(D, EXPERTS * H)
    route_values = score_all.reshape(-1)[flat_index].reshape(N_LOCAL, N_REP, COHORT, TOP).astype(jnp.float32)
    dense_grad = jnp.sum(route_hits.astype(jnp.float32) * route_values[..., None], axis=3)
    grad_route = dense_grad.reshape(N_LOCAL * N_REP * COHORT, EXPERTS).astype(jnp.bfloat16)
    return grad_gate_pre, grad_up_pre, grad_down_t, grad_route
```

```python
import functools
import jax
import jax.numpy as jnp
from jax import lax
from jax.experimental import pallas as pl
from jax.experimental.pallas import tpu as pltpu
from jax.sharding import PartitionSpec as P

H = 1024
PER_GROUP = 2
CHUNKS = 4
MESH = pl.DeviceIdType.MESH
F32 = jnp.float32
BF16 = jnp.bfloat16
KERNEL_PARAMS = dict(vmem_limit_bytes=40 * 1024 * 1024)


def contract_rows(left, right):
    return lax.dot_general(left, right, (((0,), (0,)), ((), ())), preferred_element_type=F32)


def one_hot(member, column, width):
    lanes = lax.broadcasted_iota(jnp.int32, (member.shape[0], width), 1).astype(F32)
    return jnp.where((member > 0) & (column == lanes), 1.0, 0.0).astype(BF16)


def lower_triangle(rows, block):
    row = lax.broadcasted_iota(jnp.int32, (rows, rows), 0)
    col = lax.broadcasted_iota(jnp.int32, (rows, rows), 1)
    return jnp.where((col < row) & (row // block == col // block), 1.0, 0.0).astype(BF16)


def routed_kernel(
    dims, ids_ref, rw_ref, grad_ref, gate_ref, up_ref, w_ref,
    cot_out, wtd_out, ggate_out, gup_out, route_out,
    ids_buf, rw_buf, coh, gath, peer_cot, w_buf, gate_buf, up_buf, acc, share_buf, back_buf,
    load_sem, w_sem, own_sem,
    ids_send, ids_recv, rw_send, rw_recv, coh_send, coh_recv,
    zids_send, zids_recv, zrw_send, zrw_recv,
    right_send, right_recv, left_send, left_recv,
    wtd_send, wtd_recv, cot_send, cot_recv, share_send, share_recv,
):
    nodes, locals_, tok, top, width, hs, group_tok, owners = dims
    cohort = nodes * tok
    exp_group = locals_ // owners
    slots = gate_ref.shape[0]
    capacity = slots // locals_
    half = width // 2
    cw = width // CHUNKS
    half_chunks = CHUNKS // 2
    me_n, me_l, me_r = lax.axis_index("node"), lax.axis_index("local"), lax.axis_index("rep")
    peer = {"rep": 1 - me_r}

    def node_at(k):
        return {"node": lax.rem(me_n + k, nodes)}

    def local_at(k):
        return {"local": lax.rem(me_l + k, locals_)}

    def remote(src, dst, send, recv, device):
        return pltpu.make_async_remote_copy(
            src_ref=src, dst_ref=dst, send_sem=send, recv_sem=recv,
            device_id=device, device_id_type=MESH,
        )

    barrier = pltpu.get_barrier_semaphore()
    for k in range(1, nodes):
        pl.semaphore_signal(barrier, inc=1, device_id=node_at(k), device_id_type=MESH)
    for k in range(1, locals_):
        pl.semaphore_signal(barrier, inc=1, device_id=local_at(k), device_id_type=MESH)
    pl.semaphore_signal(barrier, inc=1, device_id=peer, device_id_type=MESH)

    def cols(c):
        return pl.ds(c * cw, cw)

    own_copies = [
        pltpu.make_async_copy(ids_ref, ids_buf.at[me_l, me_n], own_sem.at[0]),
        pltpu.make_async_copy(rw_ref, rw_buf.at[me_l, me_n], own_sem.at[1]),
        pltpu.make_async_copy(grad_ref, coh.at[me_n], own_sem.at[2]),
    ]
    for copy in own_copies:
        copy.start()
    gate_copy = pltpu.make_async_copy(gate_ref, gate_buf, load_sem.at[0])
    up_copy = pltpu.make_async_copy(up_ref, up_buf, load_sem.at[1])
    gate_copy.start()
    up_copy.start()
    w_copies = [
        pltpu.make_async_copy(w_ref.at[cols(c), :], w_buf.at[cols(c), :], w_sem.at[c])
        for c in range(CHUNKS)
    ]
    pl.semaphore_wait(barrier, nodes + locals_ - 1)

    ids_copies, rw_copies, coh_copies = [], [], {}
    for k in range(1, nodes):
        ids_copies.append(remote(ids_ref, ids_buf.at[me_l, me_n], ids_send.at[k], ids_recv.at[k], node_at(k)))
        rw_copies.append(remote(rw_ref, rw_buf.at[me_l, me_n], rw_send.at[k], rw_recv.at[k], node_at(k)))
    for copy in ids_copies + rw_copies:
        copy.start()
    for c in range(CHUNKS):
        for k in range(1, nodes):
            copy = remote(
                grad_ref.at[:, cols(c)], coh.at[me_n, :, cols(c)],
                coh_send.at[c, k], coh_recv.at[c, k], node_at(k),
            )
            copy.start()
            coh_copies[c, k] = copy
    for copy in w_copies:
        copy.start()
    for copy in own_copies:
        copy.wait()
    for copy in ids_copies + rw_copies:
        copy.wait_recv()
    zids_copies, zrw_copies = [], []
    for k in range(1, locals_):
        zids_copies.append(remote(ids_buf.at[me_l], ids_buf.at[me_l], zids_send.at[k], zids_recv.at[k], local_at(k)))
        zrw_copies.append(remote(rw_buf.at[me_l], rw_buf.at[me_l], zrw_send.at[k], zrw_recv.at[k], local_at(k)))
    for copy in zids_copies + zrw_copies:
        copy.start()

    own_ids = ids_buf[me_l].reshape(cohort, top)
    lanes = lax.broadcasted_iota(jnp.int32, (cohort, 128), 1)
    first = me_n * exp_group
    hits = jnp.zeros((cohort, 128), F32)
    for k in range(top):
        hits = hits + jnp.where((own_ids[:, k:k + 1] - first == lanes) & (lanes < exp_group), 1.0, 0.0)
    in_group = jnp.where(jnp.sum(hits, axis=1, keepdims=True) > 0, 1.0, 0.0)
    hits = jnp.where(lanes == exp_group, in_group, hits)
    before = jnp.dot(lower_triangle(cohort, cohort), hits.astype(BF16), preferred_element_type=F32)
    pick = one_hot(in_group, before[:, exp_group:exp_group + 1], group_tok)

    def shifted(buf, copies_send, copies_recv, source, d, c, step):
        return remote(
            buf.at[source, :, cols(c)], buf.at[source, :, cols(c)],
            copies_send.at[d - 1, c], copies_recv.at[d - 1, c], {"local": me_l + step},
        )

    def right(source, d, c):
        return shifted(gath, right_send, right_recv, source, d, c, 1)

    def left(source, d, c):
        return shifted(gath, left_send, left_recv, source, d, c, -1)

    state = {}

    def prepare():
        for copy in zids_copies + zrw_copies:
            copy.wait_recv()
        total = locals_ * cohort
        all_ids = ids_buf[...].reshape(total, top)
        all_rw = rw_buf[...].astype(F32).reshape(total, top)
        expert = first + me_l // owners
        match = jnp.where(all_ids == expert, 1.0, 0.0)
        member = jnp.sum(match, axis=1, keepdims=True)
        row_weight = jnp.sum(match * all_rw, axis=1, keepdims=True)
        near = jnp.where((all_ids >= first) & (all_ids < first + exp_group), 1.0, 0.0)
        grouped = jnp.where(jnp.sum(near, axis=1, keepdims=True) > 0, 1.0, 0.0)
        lane = lax.broadcasted_iota(jnp.int32, (total, 128), 1)
        both = jnp.where(lane == 0, member, jnp.where(lane == 1, grouped, 0.0)).astype(BF16)
        earlier = jnp.dot(lower_triangle(total, cohort), both, preferred_element_type=F32)
        which = (lax.broadcasted_iota(jnp.int32, (total, 1), 0) // cohort).astype(F32)
        slot_hot = one_hot(member, earlier[:, 0:1] + which * capacity, slots)
        pack_hot = one_hot(grouped, earlier[:, 1:2] + which * group_tok, locals_ * group_tok)
        state["select"] = contract_rows(slot_hot, pack_hot).astype(BF16)
        weight = contract_rows(slot_hot, jnp.broadcast_to(row_weight, (total, 128)).astype(BF16))[:, 0:1]
        state["weight"] = weight
        gate_copy.wait()
        up_copy.wait()
        gate = gate_buf[...].astype(F32)
        hidden = gate * jax.nn.sigmoid(gate) * up_buf[...].astype(F32)
        wtd_out[0:slots, :] = (weight * hidden).astype(BF16)

    wtd_copy = remote(wtd_out.at[0:slots, :], wtd_out.at[slots:2 * slots, :], wtd_send, wtd_recv, peer)

    def cot_copy(c):
        part = pl.ds((c % half_chunks) * cw, cw)
        return remote(
            peer_cot.at[:, part], cot_out.at[slots:2 * slots, part],
            cot_send.at[c % half_chunks], cot_recv.at[c % half_chunks], peer,
        )

    def finish(c):
        rows = gath[:, :, cols(c)].reshape(locals_ * group_tok, cw)
        cot = jnp.dot(state["select"], rows, preferred_element_type=F32).astype(BF16)
        part = pl.ds((c % half_chunks) * cw, cw)

        @pl.when(me_r == c // half_chunks)
        def _():
            cot_out[0:slots, part] = cot

        @pl.when(me_r != c // half_chunks)
        def _():
            peer_cot[:, part] = cot

        w_copies[c].wait()
        term = jnp.dot(cot, w_buf[cols(c), :], preferred_element_type=F32)
        if c == 0:
            acc[...] = term
        else:
            acc[...] += term

        @pl.when(me_r != c // half_chunks)
        def _():
            cot_copy(c).start()

    for step in range(CHUNKS + locals_ - 1):
        if step < CHUNKS:
            for k in range(1, nodes):
                coh_copies[step, k].wait_recv()
            rows = coh[:, :, cols(step)].astype(F32).reshape(cohort, cw).astype(BF16)
            gath[me_l, :, cols(step)] = contract_rows(pick, rows).astype(BF16)

            @pl.when(me_l + 1 < locals_)
            def _():
                right(me_l, 1, step).start()

            @pl.when(me_l > 0)
            def _():
                left(me_l, 1, step).start()

        for d in range(1, locals_):
            c = step - d
            if not 0 <= c < CHUNKS:
                continue

            @pl.when(me_l >= d)
            def _():
                right(me_l - d, d, c).wait_recv()
                if d < locals_ - 1:
                    @pl.when(me_l + 1 < locals_)
                    def _():
                        right(me_l - d, d + 1, c).start()

            @pl.when(me_l + d < locals_)
            def _():
                left(me_l + d, d, c).wait_recv()
                if d < locals_ - 1:
                    @pl.when(me_l > 0)
                    def _():
                        left(me_l + d, d + 1, c).start()

        if step == locals_ - 2:
            prepare()
        if step >= locals_ - 1:
            finish(step - locals_ + 1)
            if step == locals_ - 1:
                wtd_copy.start()

    weight = state["weight"]
    gate = gate_buf[...].astype(F32)
    up = up_buf[...].astype(F32)
    back = acc[...]
    sig = jax.nn.sigmoid(gate)
    act = gate * sig
    shares = jnp.sum(act * up * back, axis=1, keepdims=True)
    share_buf[...] = jnp.broadcast_to(shares, (slots, 128)).astype(BF16).reshape(locals_, capacity, 128)
    scaled = weight * back
    ggate_out[...] = (scaled * up * sig * (1.0 + gate * (1.0 - sig))).astype(BF16)
    gup_out[...] = (scaled * act).astype(BF16)
    back_buf[me_l] = share_buf[me_l]
    share_copies = [
        remote(share_buf.at[lax.rem(me_l + k, locals_)], back_buf.at[me_l], share_send.at[k], share_recv.at[k], local_at(k))
        for k in range(1, locals_)
    ]
    for copy in share_copies:
        copy.start()

    for copy in ids_copies + rw_copies + zids_copies + zrw_copies + list(coh_copies.values()):
        copy.wait_send()
    for c in range(CHUNKS):
        @pl.when(me_l + 1 < locals_)
        def _():
            for d in range(locals_ - 1):
                @pl.when(me_l >= d)
                def _():
                    right(me_l - d, d + 1, c).wait_send()

        @pl.when(me_l > 0)
        def _():
            for d in range(locals_ - 1):
                @pl.when(me_l + d < locals_)
                def _():
                    left(me_l + d, d + 1, c).wait_send()
    wtd_copy.wait()
    for c in range(half_chunks):
        cot_copy(c).wait()
    for copy in share_copies:
        copy.wait()
    route = jnp.zeros((cohort, 128), F32)
    for j in range(exp_group):
        chosen = one_hot(hits[:, j:j + 1], before[:, j:j + 1], capacity)
        value = jnp.zeros((cohort, 128), F32)
        for o in range(owners):
            value = value + jnp.dot(chosen, back_buf[j * owners + o], preferred_element_type=F32)
        route = jnp.where(lanes == j, value, route)
    route_out[...] = route[:, 0:exp_group].astype(BF16)


def gathered(nodes, locals_, group_tok, grad_out, expert_ids, route_weights, gate_pre, up_pre, w_down_t):
    tok, width = grad_out.shape
    top = expert_ids.shape[1]
    slots, hs = gate_pre.shape
    owners = H // hs
    exp_group = locals_ // owners
    cohort = nodes * tok
    capacity = slots // locals_
    half = width // 2
    dims = (nodes, locals_, tok, top, width, hs, group_tok, owners)
    dma = pltpu.SemaphoreType.DMA
    cot, weighted, grad_gate, grad_up, grad_route = pl.pallas_call(
        functools.partial(routed_kernel, dims),
        out_shape=(
            jax.ShapeDtypeStruct((2 * slots, half), BF16),
            jax.ShapeDtypeStruct((2 * slots, hs), BF16),
            jax.ShapeDtypeStruct((slots, hs), BF16),
            jax.ShapeDtypeStruct((slots, hs), BF16),
            jax.ShapeDtypeStruct((cohort, exp_group), BF16),
        ),
        in_specs=[pl.BlockSpec(memory_space=pl.ANY)] * 6,
        out_specs=tuple([pl.BlockSpec(memory_space=pltpu.VMEM)] * 5),
        scratch_shapes=[
            pltpu.VMEM((locals_, nodes, tok, top), jnp.int32),
            pltpu.VMEM((locals_, nodes, tok, top), BF16),
            pltpu.VMEM((nodes, tok, width), BF16),
            pltpu.VMEM((locals_, group_tok, width), BF16),
            pltpu.VMEM((slots, half), BF16),
            pltpu.VMEM((width, hs), BF16),
            pltpu.VMEM((slots, hs), BF16),
            pltpu.VMEM((slots, hs), BF16),
            pltpu.VMEM((slots, hs), F32),
            pltpu.VMEM((locals_, capacity, 128), BF16),
            pltpu.VMEM((locals_, capacity, 128), BF16),
            dma((2,)), dma((CHUNKS,)), dma((3,)),
            dma((nodes,)), dma((nodes,)), dma((nodes,)), dma((nodes,)),
            dma((CHUNKS, nodes)), dma((CHUNKS, nodes)),
            dma((locals_,)), dma((locals_,)), dma((locals_,)), dma((locals_,)),
            dma((locals_ - 1, CHUNKS)), dma((locals_ - 1, CHUNKS)),
            dma((locals_ - 1, CHUNKS)), dma((locals_ - 1, CHUNKS)),
            dma(()), dma(()), dma((CHUNKS // 2,)), dma((CHUNKS // 2,)),
            dma((locals_,)), dma((locals_,)),
        ],
        compiler_params=pltpu.CompilerParams(collective_id=0, has_side_effects=True, **KERNEL_PARAMS),
        name="routed",
    )(expert_ids, route_weights, grad_out, gate_pre, up_pre, w_down_t)
    grad_down = contract_rows(cot, weighted).astype(BF16)
    return grad_gate, grad_up, grad_down, grad_route


def swapped(block, axis, distance):
    count = lax.axis_size(axis)
    route = []
    for low in range(count):
        high = low | 1 << distance
        if high != low and high < count:
            route += [(low, high), (high, low)]
    return lax.ppermute(block, axis, route)


def outer_term(columns, weighted):
    return lax.dot_general(
        columns, weighted, (((0,), (0,)), ((), ())), preferred_element_type=jnp.float32
    )


def exchanged(grad_out, expert_ids, route_weights, gate_pre, up_pre, w_down_t):
    tok_dev, width = grad_out.shape
    slot_rows, hidden_slice = gate_pre.shape
    node_count = lax.axis_size("node")
    local_count = lax.axis_size("local")
    owners = H // hidden_slice
    exp_group = local_count // owners
    experts = exp_group * node_count
    capacity = slot_rows // local_count
    expert_range = lax.iota(jnp.int32, experts)
    route_hits = expert_ids[:, :, None] == expert_range[None, None, :]
    dense_weights = jnp.sum(
        jnp.where(route_hits, route_weights[:, :, None].astype(jnp.float32), 0.0), axis=1
    ).astype(jnp.bfloat16)
    cohort_grad, cohort_weights = (
        lax.all_gather(grad_out, "node", axis=0, tiled=True),
        lax.all_gather(dense_weights, "node", axis=0, tiled=True),
    )
    group_index = lax.axis_index("node")
    group_weights = lax.dynamic_slice_in_dim(cohort_weights, group_index * exp_group, exp_group, 1)
    routed = (group_weights != 0).astype(jnp.int32)
    earlier = jnp.cumsum(routed, axis=0) - routed
    slot_range = lax.iota(jnp.int32, capacity)
    select = (routed[:, :, None] == 1) & (earlier[:, :, None] == slot_range[None, None, :])
    select_half = select.astype(jnp.bfloat16)
    packed = jnp.einsum(
        "cjs,cd->jsd", select_half, cohort_grad, preferred_element_type=jnp.float32
    ).astype(jnp.bfloat16)
    packed_weights = jnp.einsum(
        "cjs,cj->js", select_half, group_weights, preferred_element_type=jnp.float32
    ).astype(jnp.bfloat16)
    send_grad = jnp.broadcast_to(packed[:, None], (exp_group, owners, capacity, width)).reshape(
        local_count, capacity, width
    )
    send_weights = jnp.broadcast_to(packed_weights[:, None], (exp_group, owners, capacity)).reshape(
        local_count, capacity
    )
    recv_grad, recv_weights = (
        lax.all_to_all(send_grad, "local", split_axis=0, concat_axis=0, tiled=True),
        lax.all_to_all(send_weights, "local", split_axis=0, concat_axis=0, tiled=True),
    )
    cotangent = recv_grad.reshape(slot_rows, width)
    weight = recv_weights.reshape(slot_rows, 1).astype(jnp.float32)
    gate_value = gate_pre.astype(jnp.float32)
    up_value = up_pre.astype(jnp.float32)
    backward = jnp.dot(cotangent, w_down_t, preferred_element_type=jnp.float32)
    sigmoid_gate = jax.nn.sigmoid(gate_value)
    activated = gate_value * sigmoid_gate
    hidden = activated * up_value
    shares = jnp.sum(hidden * backward, axis=1).astype(jnp.bfloat16)
    scaled = weight * backward
    grad_gate_pre = (
        scaled * up_value * sigmoid_gate * (1.0 + gate_value * (1.0 - sigmoid_gate))
    ).astype(jnp.bfloat16)
    grad_up_pre = (scaled * activated).astype(jnp.bfloat16)
    weighted = (weight * hidden).astype(jnp.bfloat16)
    returned = lax.all_to_all(
        shares.reshape(local_count, capacity), "local", split_axis=0, concat_axis=0, tiled=True
    )
    slice_sum = jnp.sum(returned.astype(jnp.float32).reshape(exp_group, owners, capacity), axis=1)
    grad_route = jnp.sum(jnp.where(select, slice_sum[None], 0.0), axis=2).astype(jnp.bfloat16)
    half_width = width // lax.axis_size("rep")
    replica = lax.axis_index("rep")
    own_cols = lax.dynamic_slice_in_dim(cotangent, replica * half_width, half_width, 1)
    peer_cols = lax.dynamic_slice_in_dim(cotangent, (1 - replica) * half_width, half_width, 1)
    got_cols, got_weighted = swapped((peer_cols, weighted), "rep", 0)
    own_term = outer_term(own_cols, weighted).astype(jnp.bfloat16).astype(jnp.float32)
    peer_term = outer_term(got_cols, got_weighted).astype(jnp.bfloat16).astype(jnp.float32)
    grad_down_t = (own_term + peer_term).astype(jnp.bfloat16)
    return (grad_gate_pre, grad_up_pre, grad_down_t, grad_route)


def per_device(grad_out, expert_ids, route_weights, gate_pre, up_pre, w_down_t):
    nodes, locals_ = lax.axis_size("node"), lax.axis_size("local")
    capacity = gate_pre.shape[0] // locals_
    group_tok = grad_out.shape[0] * expert_ids.shape[1] // PER_GROUP
    args = (grad_out, expert_ids, route_weights, gate_pre, up_pre, w_down_t)
    if group_tok > capacity:
        return exchanged(*args)
    return gathered(nodes, locals_, group_tok, *args)


def solution(mesh):
    placed = (
        P(("node", "local", "rep"), None),
        P(("node", "local", "rep"), None),
        P(("node", "local", "rep"), None),
        P("rep", ("node", "local")),
        P("rep", ("node", "local")),
        P(None, ("node", "local")),
    )
    return jax.shard_map(
        per_device,
        mesh=mesh,
        in_specs=placed,
        out_specs=(
            P("rep", ("node", "local")),
            P("rep", ("node", "local")),
            P("rep", ("node", "local")),
            P(("local", "rep"), "node"),
        ),
        check_vma=False,
    )
```

```python
import functools
import jax
import jax.numpy as jnp
from jax import lax
from jax.experimental import pallas as pl
from jax.experimental.pallas import tpu as pltpu
from jax.sharding import PartitionSpec as P

H = 1024
PER_GROUP = 2
CHUNKS = 4
DOWN_STEPS = 8
MESH = pl.DeviceIdType.MESH
F32 = jnp.float32
BF16 = jnp.bfloat16
KERNEL_PARAMS = dict(vmem_limit_bytes=40 * 1024 * 1024)


def contract_rows(left, right):
    return lax.dot_general(left, right, (((0,), (0,)), ((), ())), preferred_element_type=F32)


def one_hot(member, row, height):
    places = lax.broadcasted_iota(jnp.int32, (height, member.shape[1]), 0).astype(F32)
    return jnp.where((member > 0) & (row == places), 1.0, 0.0)


def earlier_counts(rows, block):
    count = rows.shape[1]
    above = lax.broadcasted_iota(jnp.int32, (count, count), 0)
    col = lax.broadcasted_iota(jnp.int32, (count, count), 1)
    strict = jnp.where((above < col) & (above // block == col // block), 1.0, 0.0).astype(BF16)
    return jnp.dot(rows.astype(BF16), strict, preferred_element_type=F32)


def stacked(rows):
    lines = lax.broadcasted_iota(jnp.int32, (8, rows[0].shape[1]), 0)
    out = jnp.zeros(lines.shape, F32)
    for place, row in enumerate(rows):
        out = jnp.where(lines == place, row, out)
    return out


def routed_kernel(
    dims, ids_ref, rw_ref, grad_ref, gate_ref, up_ref, w_ref,
    cot_out, wtd_out, back_out, weight_out, route_out,
    ids_buf, rw_buf, coh, gath, peer_cot, w_buf, gate_buf, up_buf, acc, hidden_buf, share_buf, back_buf,
    load_sem, w_sem, own_sem,
    ids_send, ids_recv, rw_send, rw_recv, coh_send, coh_recv,
    zids_send, zids_recv, zrw_send, zrw_recv,
    right_send, right_recv, left_send, left_recv,
    wtd_send, wtd_recv, cot_send, cot_recv, share_send, share_recv,
):
    nodes, locals_, tok, top, width, hs, group_tok, owners = dims
    cohort = nodes * tok
    exp_group = locals_ // owners
    slots = gate_ref.shape[0]
    capacity = slots // locals_
    half = width // 2
    cw = width // CHUNKS
    half_chunks = CHUNKS // 2
    me_n, me_l, me_r = lax.axis_index("node"), lax.axis_index("local"), lax.axis_index("rep")
    peer = {"rep": 1 - me_r}

    def node_at(k):
        return {"node": lax.rem(me_n + k, nodes)}

    def local_at(k):
        return {"local": lax.rem(me_l + k, locals_)}

    def remote(src, dst, send, recv, device):
        return pltpu.make_async_remote_copy(
            src_ref=src, dst_ref=dst, send_sem=send, recv_sem=recv,
            device_id=device, device_id_type=MESH,
        )

    barrier = pltpu.get_barrier_semaphore()
    for k in range(1, nodes):
        pl.semaphore_signal(barrier, inc=1, device_id=node_at(k), device_id_type=MESH)
    for k in range(1, locals_):
        pl.semaphore_signal(barrier, inc=1, device_id=local_at(k), device_id_type=MESH)
    pl.semaphore_signal(barrier, inc=1, device_id=peer, device_id_type=MESH)

    def cols(c):
        return pl.ds(c * cw, cw)

    own_copies = [
        pltpu.make_async_copy(ids_ref, ids_buf.at[me_l, me_n], own_sem.at[0]),
        pltpu.make_async_copy(rw_ref, rw_buf.at[me_l, me_n], own_sem.at[1]),
        pltpu.make_async_copy(grad_ref, coh.at[me_n], own_sem.at[2]),
    ]
    for copy in own_copies:
        copy.start()
    gate_copy = pltpu.make_async_copy(gate_ref, gate_buf, load_sem.at[0])
    up_copy = pltpu.make_async_copy(up_ref, up_buf, load_sem.at[1])
    gate_copy.start()
    up_copy.start()
    w_copies = [
        pltpu.make_async_copy(w_ref.at[cols(c), :], w_buf.at[cols(c), :], w_sem.at[c])
        for c in range(CHUNKS)
    ]
    pl.semaphore_wait(barrier, nodes + locals_ - 1)

    meta_copies, coh_copies = [], {}
    for k in range(1, nodes):
        meta_copies.append(remote(ids_ref, ids_buf.at[me_l, me_n], ids_send.at[k], ids_recv.at[k], node_at(k)))
        meta_copies.append(remote(rw_ref, rw_buf.at[me_l, me_n], rw_send.at[k], rw_recv.at[k], node_at(k)))
    for copy in meta_copies:
        copy.start()
    for c in range(CHUNKS):
        for k in range(1, nodes):
            copy = remote(
                grad_ref.at[:, cols(c)], coh.at[me_n, :, cols(c)],
                coh_send.at[c, k], coh_recv.at[c, k], node_at(k),
            )
            copy.start()
            coh_copies[c, k] = copy
    for copy in w_copies:
        copy.start()
    for copy in own_copies:
        copy.wait()
    for copy in meta_copies:
        copy.wait_recv()
    zmeta_copies = []
    for k in range(1, locals_):
        zmeta_copies.append(remote(ids_buf.at[me_l], ids_buf.at[me_l], zids_send.at[k], zids_recv.at[k], local_at(k)))
        zmeta_copies.append(remote(rw_buf.at[me_l], rw_buf.at[me_l], zrw_send.at[k], zrw_recv.at[k], local_at(k)))
    for copy in zmeta_copies:
        copy.start()

    own = ids_buf[me_l].astype(F32)
    own_ids = jnp.concatenate([own[n] for n in range(nodes)], axis=1)
    first = me_n * exp_group
    low = first.astype(F32)
    hits = [
        jnp.sum(jnp.where(own_ids == low + j, 1.0, 0.0), axis=0, keepdims=True)
        for j in range(exp_group)
    ]
    in_group = jnp.where(sum(hits) > 0, 1.0, 0.0)
    before = earlier_counts(stacked(hits + [in_group]), cohort)
    pick = one_hot(in_group, before[exp_group:exp_group + 1], group_tok).astype(BF16)

    def shifted(buf, copies_send, copies_recv, source, d, c, step):
        return remote(
            buf.at[source, :, cols(c)], buf.at[source, :, cols(c)],
            copies_send.at[d - 1, c], copies_recv.at[d - 1, c], {"local": me_l + step},
        )

    def right(source, d, c):
        return shifted(gath, right_send, right_recv, source, d, c, 1)

    def left(source, d, c):
        return shifted(gath, left_send, left_recv, source, d, c, -1)

    state = {}

    def prepare():
        for copy in zmeta_copies:
            copy.wait_recv()
        total = locals_ * cohort
        ids_all, rw_all = ids_buf[...].astype(F32), rw_buf[...].astype(F32)
        places = [(l, n) for l in range(locals_) for n in range(nodes)]
        all_ids = jnp.concatenate([ids_all[place] for place in places], axis=1)
        all_rw = jnp.concatenate([rw_all[place] for place in places], axis=1)
        match = jnp.where(all_ids == (first + me_l // owners).astype(F32), 1.0, 0.0)
        member = jnp.sum(match, axis=0, keepdims=True)
        row_weight = jnp.sum(match * all_rw, axis=0, keepdims=True)
        near = jnp.where((all_ids >= low) & (all_ids < low + exp_group), 1.0, 0.0)
        grouped = jnp.where(jnp.sum(near, axis=0, keepdims=True) > 0, 1.0, 0.0)
        earlier = earlier_counts(stacked([member, grouped]), cohort)
        which = (lax.broadcasted_iota(jnp.int32, (1, total), 1) // cohort).astype(F32)
        slot_hot = one_hot(member, earlier[0:1] + which * capacity, slots)
        pack_hot = one_hot(grouped, earlier[1:2] + which * group_tok, locals_ * group_tok)
        state["select"] = lax.dot_general(
            slot_hot.astype(BF16), pack_hot.astype(BF16),
            (((1,), (1,)), ((), ())), preferred_element_type=F32,
        ).astype(BF16)
        weight = jnp.sum(slot_hot * row_weight, axis=1, keepdims=True)
        weight_out[...] = jnp.broadcast_to(weight, (slots, 128))
        gate_copy.wait()
        up_copy.wait()
        gate = gate_buf[...].astype(F32)
        hidden = gate * jax.nn.sigmoid(gate) * up_buf[...].astype(F32)
        hidden_buf[...] = hidden
        wtd_out[0:slots, :] = (weight * hidden).astype(BF16)

    wtd_copy = remote(wtd_out.at[0:slots, :], wtd_out.at[slots:2 * slots, :], wtd_send, wtd_recv, peer)

    def cot_copy(c):
        part = pl.ds((c % half_chunks) * cw, cw)
        return remote(
            peer_cot.at[:, part], cot_out.at[slots:2 * slots, part],
            cot_send.at[c % half_chunks], cot_recv.at[c % half_chunks], peer,
        )

    def finish(c):
        rows = gath[:, :, cols(c)].reshape(locals_ * group_tok, cw)
        cot = jnp.dot(state["select"], rows, preferred_element_type=F32).astype(BF16)
        part = pl.ds((c % half_chunks) * cw, cw)

        @pl.when(me_r == c // half_chunks)
        def _():
            cot_out[0:slots, part] = cot

        @pl.when(me_r != c // half_chunks)
        def _():
            peer_cot[:, part] = cot

        w_copies[c].wait()
        term = jnp.dot(cot, w_buf[cols(c), :], preferred_element_type=F32)
        if c == 0:
            acc[...] = term
        else:
            acc[...] += term

        @pl.when(me_r != c // half_chunks)
        def _():
            cot_copy(c).start()

    for step in range(CHUNKS + locals_ - 1):
        if step < CHUNKS:
            for k in range(1, nodes):
                coh_copies[step, k].wait_recv()
            rows = coh[:, :, cols(step)].astype(F32).reshape(cohort, cw).astype(BF16)
            packed = jnp.dot(pick, rows, preferred_element_type=F32)
            gath[me_l, :, cols(step)] = packed.astype(BF16)

            @pl.when(me_l + 1 < locals_)
            def _():
                right(me_l, 1, step).start()

            @pl.when(me_l > 0)
            def _():
                left(me_l, 1, step).start()

        for d in range(1, locals_):
            c = step - d
            if not 0 <= c < CHUNKS:
                continue

            @pl.when(me_l >= d)
            def _():
                right(me_l - d, d, c).wait_recv()
                if d < locals_ - 1:
                    @pl.when(me_l + 1 < locals_)
                    def _():
                        right(me_l - d, d + 1, c).start()

            @pl.when(me_l + d < locals_)
            def _():
                left(me_l + d, d, c).wait_recv()
                if d < locals_ - 1:
                    @pl.when(me_l > 0)
                    def _():
                        left(me_l + d, d + 1, c).start()

        if step == locals_ - 2:
            prepare()
        if step >= locals_ - 1:
            finish(step - locals_ + 1)
            if step == locals_ - 1:
                wtd_copy.start()

    back = acc[...]
    shares = jnp.sum(hidden_buf[...] * back, axis=1, keepdims=True)
    share_buf[...] = jnp.broadcast_to(shares, (slots, 128)).astype(BF16).reshape(locals_, capacity, 128)
    back_buf[me_l] = share_buf[me_l]
    share_copies = [
        remote(share_buf.at[lax.rem(me_l + k, locals_)], back_buf.at[me_l], share_send.at[k], share_recv.at[k], local_at(k))
        for k in range(1, locals_)
    ]
    for copy in share_copies:
        copy.start()
    back_out[...] = back

    for copy in meta_copies + zmeta_copies + list(coh_copies.values()):
        copy.wait_send()
    for c in range(CHUNKS):
        @pl.when(me_l + 1 < locals_)
        def _():
            for d in range(locals_ - 1):
                @pl.when(me_l >= d)
                def _():
                    right(me_l - d, d + 1, c).wait_send()

        @pl.when(me_l > 0)
        def _():
            for d in range(locals_ - 1):
                @pl.when(me_l + d < locals_)
                def _():
                    left(me_l + d, d + 1, c).wait_send()
    wtd_copy.wait()
    for c in range(half_chunks):
        cot_copy(c).wait()
    for copy in share_copies:
        copy.wait()
    route = []
    for j in range(exp_group):
        chosen = one_hot(hits[j], before[j:j + 1], capacity)
        value = jnp.zeros((capacity, 1), F32)
        for o in range(owners):
            value = value + back_buf[j * owners + o, :, 0:1].astype(F32)
        route.append(jnp.sum(chosen * value, axis=0, keepdims=True))
    route_out[...] = stacked(route)


def gradient_kernel(exp_group, cot, wtd, back_in, weight, route, gate_in, up_in, ggate, gup, down, groute):
    down[...] = contract_rows(cot[...], wtd[...]).astype(BF16)

    @pl.when(pl.program_id(0) == 0)
    def _():
        gate = gate_in[...].astype(F32)
        sig = jax.nn.sigmoid(gate)
        scaled = weight[:, 0:1] * back_in[...]
        ggate[...] = (scaled * up_in[...].astype(F32) * sig * (1.0 + gate * (1.0 - sig))).astype(BF16)
        gup[...] = (scaled * gate * sig).astype(BF16)
        groute[...] = route[0:exp_group, :].astype(BF16)


def gathered(nodes, locals_, group_tok, grad_out, expert_ids, route_weights, gate_pre, up_pre, w_down_t):
    tok, width = grad_out.shape
    top = expert_ids.shape[1]
    slots, hs = gate_pre.shape
    owners = H // hs
    exp_group = locals_ // owners
    cohort = nodes * tok
    capacity = slots // locals_
    half = width // 2
    dims = (nodes, locals_, tok, top, width, hs, group_tok, owners)
    dma = pltpu.SemaphoreType.DMA
    hbm = pl.BlockSpec(memory_space=pltpu.HBM)
    cot, weighted, back, weight, route = pl.pallas_call(
        functools.partial(routed_kernel, dims),
        out_shape=(
            jax.ShapeDtypeStruct((2 * slots, half), BF16),
            jax.ShapeDtypeStruct((2 * slots, hs), BF16),
            jax.ShapeDtypeStruct((slots, hs), F32),
            jax.ShapeDtypeStruct((slots, 128), F32),
            jax.ShapeDtypeStruct((8, cohort), F32),
        ),
        in_specs=[hbm] * 6,
        out_specs=tuple([pl.BlockSpec(memory_space=pltpu.VMEM)] * 5),
        scratch_shapes=[
            pltpu.VMEM((locals_, nodes, top, tok), jnp.int32),
            pltpu.VMEM((locals_, nodes, top, tok), BF16),
            pltpu.VMEM((nodes, tok, width), BF16),
            pltpu.VMEM((locals_, group_tok, width), BF16),
            pltpu.VMEM((slots, half), BF16),
            pltpu.VMEM((width, hs), BF16),
            pltpu.VMEM((slots, hs), BF16),
            pltpu.VMEM((slots, hs), BF16),
            pltpu.VMEM((slots, hs), F32),
            pltpu.VMEM((slots, hs), F32),
            pltpu.VMEM((locals_, capacity, 128), BF16),
            pltpu.VMEM((locals_, capacity, 128), BF16),
            dma((2,)), dma((CHUNKS,)), dma((3,)),
            dma((nodes,)), dma((nodes,)), dma((nodes,)), dma((nodes,)),
            dma((CHUNKS, nodes)), dma((CHUNKS, nodes)),
            dma((locals_,)), dma((locals_,)), dma((locals_,)), dma((locals_,)),
            dma((locals_ - 1, CHUNKS)), dma((locals_ - 1, CHUNKS)),
            dma((locals_ - 1, CHUNKS)), dma((locals_ - 1, CHUNKS)),
            dma(()), dma(()), dma((CHUNKS // 2,)), dma((CHUNKS // 2,)),
            dma((locals_,)), dma((locals_,)),
        ],
        compiler_params=pltpu.CompilerParams(collective_id=0, has_side_effects=True, **KERNEL_PARAMS),
        name="routed",
    )(*[
        pltpu.with_memory_space_constraint(x, pltpu.HBM)
        for x in (expert_ids.T, route_weights.T, grad_out, gate_pre, up_pre, w_down_t)
    ])
    tile = half // DOWN_STEPS
    vmem = pl.BlockSpec(memory_space=pltpu.VMEM)
    grad_gate, grad_up, grad_down, grad_route = pl.pallas_call(
        functools.partial(gradient_kernel, exp_group),
        grid=(DOWN_STEPS,),
        out_shape=(
            jax.ShapeDtypeStruct((slots, hs), BF16),
            jax.ShapeDtypeStruct((slots, hs), BF16),
            jax.ShapeDtypeStruct((half, hs), BF16),
            jax.ShapeDtypeStruct((exp_group, cohort), BF16),
        ),
        in_specs=[
            pl.BlockSpec((2 * slots, tile), lambda i: (0, i)),
            vmem, vmem, vmem, vmem, vmem, vmem,
        ],
        out_specs=(
            pl.BlockSpec((slots, hs), lambda i: (0, 0)),
            pl.BlockSpec((slots, hs), lambda i: (0, 0)),
            pl.BlockSpec((tile, hs), lambda i: (i, 0)),
            pl.BlockSpec((exp_group, cohort), lambda i: (0, 0)),
        ),
        compiler_params=pltpu.CompilerParams(vmem_limit_bytes=24 * 1024 * 1024),
        name="gradients",
    )(cot, weighted, back, weight, route, gate_pre, up_pre)
    return grad_gate, grad_up, grad_down, grad_route.T


def swapped(block, axis, distance):
    count = lax.axis_size(axis)
    route = []
    for low in range(count):
        high = low | 1 << distance
        if high != low and high < count:
            route += [(low, high), (high, low)]
    return lax.ppermute(block, axis, route)


def outer_term(columns, weighted):
    return lax.dot_general(
        columns, weighted, (((0,), (0,)), ((), ())), preferred_element_type=jnp.float32
    )


def exchanged(grad_out, expert_ids, route_weights, gate_pre, up_pre, w_down_t):
    tok_dev, width = grad_out.shape
    slot_rows, hidden_slice = gate_pre.shape
    node_count = lax.axis_size("node")
    local_count = lax.axis_size("local")
    owners = H // hidden_slice
    exp_group = local_count // owners
    experts = exp_group * node_count
    capacity = slot_rows // local_count
    expert_range = lax.iota(jnp.int32, experts)
    route_hits = expert_ids[:, :, None] == expert_range[None, None, :]
    dense_weights = jnp.sum(
        jnp.where(route_hits, route_weights[:, :, None].astype(jnp.float32), 0.0), axis=1
    ).astype(jnp.bfloat16)
    cohort_grad, cohort_weights = (
        lax.all_gather(grad_out, "node", axis=0, tiled=True),
        lax.all_gather(dense_weights, "node", axis=0, tiled=True),
    )
    group_index = lax.axis_index("node")
    group_weights = lax.dynamic_slice_in_dim(cohort_weights, group_index * exp_group, exp_group, 1)
    routed = (group_weights != 0).astype(jnp.int32)
    earlier = jnp.cumsum(routed, axis=0) - routed
    slot_range = lax.iota(jnp.int32, capacity)
    select = (routed[:, :, None] == 1) & (earlier[:, :, None] == slot_range[None, None, :])
    select_half = select.astype(jnp.bfloat16)
    packed = jnp.einsum(
        "cjs,cd->jsd", select_half, cohort_grad, preferred_element_type=jnp.float32
    ).astype(jnp.bfloat16)
    packed_weights = jnp.einsum(
        "cjs,cj->js", select_half, group_weights, preferred_element_type=jnp.float32
    ).astype(jnp.bfloat16)
    send_grad = jnp.broadcast_to(packed[:, None], (exp_group, owners, capacity, width)).reshape(
        local_count, capacity, width
    )
    send_weights = jnp.broadcast_to(packed_weights[:, None], (exp_group, owners, capacity)).reshape(
        local_count, capacity
    )
    recv_grad, recv_weights = (
        lax.all_to_all(send_grad, "local", split_axis=0, concat_axis=0, tiled=True),
        lax.all_to_all(send_weights, "local", split_axis=0, concat_axis=0, tiled=True),
    )
    cotangent = recv_grad.reshape(slot_rows, width)
    weight = recv_weights.reshape(slot_rows, 1).astype(jnp.float32)
    gate_value = gate_pre.astype(jnp.float32)
    up_value = up_pre.astype(jnp.float32)
    backward = jnp.dot(cotangent, w_down_t, preferred_element_type=jnp.float32)
    sigmoid_gate = jax.nn.sigmoid(gate_value)
    activated = gate_value * sigmoid_gate
    hidden = activated * up_value
    shares = jnp.sum(hidden * backward, axis=1).astype(jnp.bfloat16)
    scaled = weight * backward
    grad_gate_pre = (
        scaled * up_value * sigmoid_gate * (1.0 + gate_value * (1.0 - sigmoid_gate))
    ).astype(jnp.bfloat16)
    grad_up_pre = (scaled * activated).astype(jnp.bfloat16)
    weighted = (weight * hidden).astype(jnp.bfloat16)
    returned = lax.all_to_all(
        shares.reshape(local_count, capacity), "local", split_axis=0, concat_axis=0, tiled=True
    )
    slice_sum = jnp.sum(returned.astype(jnp.float32).reshape(exp_group, owners, capacity), axis=1)
    grad_route = jnp.sum(jnp.where(select, slice_sum[None], 0.0), axis=2).astype(jnp.bfloat16)
    half_width = width // lax.axis_size("rep")
    replica = lax.axis_index("rep")
    own_cols = lax.dynamic_slice_in_dim(cotangent, replica * half_width, half_width, 1)
    peer_cols = lax.dynamic_slice_in_dim(cotangent, (1 - replica) * half_width, half_width, 1)
    got_cols, got_weighted = swapped((peer_cols, weighted), "rep", 0)
    own_term = outer_term(own_cols, weighted).astype(jnp.bfloat16).astype(jnp.float32)
    peer_term = outer_term(got_cols, got_weighted).astype(jnp.bfloat16).astype(jnp.float32)
    grad_down_t = (own_term + peer_term).astype(jnp.bfloat16)
    return (grad_gate_pre, grad_up_pre, grad_down_t, grad_route)


def per_device(grad_out, expert_ids, route_weights, gate_pre, up_pre, w_down_t):
    nodes, locals_ = lax.axis_size("node"), lax.axis_size("local")
    capacity = gate_pre.shape[0] // locals_
    group_tok = grad_out.shape[0] * expert_ids.shape[1] // PER_GROUP
    args = (grad_out, expert_ids, route_weights, gate_pre, up_pre, w_down_t)
    if group_tok > capacity:
        return exchanged(*args)
    return gathered(nodes, locals_, group_tok, *args)


def solution(mesh):
    placed = (
        P(("node", "local", "rep"), None),
        P(("node", "local", "rep"), None),
        P(("node", "local", "rep"), None),
        P("rep", ("node", "local")),
        P("rep", ("node", "local")),
        P(None, ("node", "local")),
    )
    return jax.shard_map(
        per_device,
        mesh=mesh,
        in_specs=placed,
        out_specs=(
            P("rep", ("node", "local")),
            P("rep", ("node", "local")),
            P("rep", ("node", "local")),
            P(("local", "rep"), "node"),
        ),
        check_vma=False,
    )
```

```python
import functools
import jax
import jax.numpy as jnp
from jax import lax
from jax.experimental import pallas as pl
from jax.experimental.pallas import tpu as pltpu
from jax.sharding import PartitionSpec as P

H = 1024
PER_GROUP = 2
CHUNKS = 4
TILES = 4
MESH = pl.DeviceIdType.MESH
F32 = jnp.float32
BF16 = jnp.bfloat16
KERNEL_PARAMS = dict(vmem_limit_bytes=40 * 1024 * 1024)


def contract_rows(left, right):
    return lax.dot_general(left, right, (((0,), (0,)), ((), ())), preferred_element_type=F32)


def one_hot(member, row, height):
    places = lax.broadcasted_iota(jnp.int32, (height, member.shape[1]), 0).astype(F32)
    return jnp.where((member > 0) & (row == places), 1.0, 0.0)


def earlier_counts(rows, block):
    count = rows.shape[1]
    above = lax.broadcasted_iota(jnp.int32, (count, count), 0)
    col = lax.broadcasted_iota(jnp.int32, (count, count), 1)
    strict = jnp.where((above < col) & (above // block == col // block), 1.0, 0.0).astype(BF16)
    return jnp.dot(rows.astype(BF16), strict, preferred_element_type=F32)


def stacked(rows):
    lines = lax.broadcasted_iota(jnp.int32, (8, rows[0].shape[1]), 0)
    out = jnp.zeros(lines.shape, F32)
    for place, row in enumerate(rows):
        out = jnp.where(lines == place, row, out)
    return out


def routed_kernel(
    dims, ids_ref, rw_ref, grad_ref, gate_ref, up_ref, w_ref,
    ggate_out, gup_out, down_out, route_out,
    cot_out, wtd_out, ids_buf, rw_buf, coh, gath, peer_cot, w_buf, gate_buf, up_buf, acc, hidden_buf, share_buf, back_buf,
    load_sem, w_sem, own_sem,
    ids_send, ids_recv, rw_send, rw_recv, coh_send, coh_recv,
    zids_send, zids_recv, zrw_send, zrw_recv,
    right_send, right_recv, left_send, left_recv,
    wtd_send, wtd_recv, cot_send, cot_recv, share_send, share_recv,
):
    nodes, locals_, tok, top, width, hs, group_tok, owners = dims
    cohort = nodes * tok
    exp_group = locals_ // owners
    slots = gate_ref.shape[0]
    capacity = slots // locals_
    half = width // 2
    cw = width // CHUNKS
    half_chunks = CHUNKS // 2
    me_n, me_l, me_r = lax.axis_index("node"), lax.axis_index("local"), lax.axis_index("rep")
    peer = {"rep": 1 - me_r}

    def node_at(k):
        return {"node": lax.rem(me_n + k, nodes)}

    def local_at(k):
        return {"local": lax.rem(me_l + k, locals_)}

    def remote(src, dst, send, recv, device):
        return pltpu.make_async_remote_copy(
            src_ref=src, dst_ref=dst, send_sem=send, recv_sem=recv,
            device_id=device, device_id_type=MESH,
        )

    barrier = pltpu.get_barrier_semaphore()
    for k in range(1, nodes):
        pl.semaphore_signal(barrier, inc=1, device_id=node_at(k), device_id_type=MESH)
    for k in range(1, locals_):
        pl.semaphore_signal(barrier, inc=1, device_id=local_at(k), device_id_type=MESH)
    pl.semaphore_signal(barrier, inc=1, device_id=peer, device_id_type=MESH)

    def cols(c):
        return pl.ds((c % 2) * half + (c // 2) * cw, cw)

    own_copies = [
        pltpu.make_async_copy(ids_ref, ids_buf.at[me_l, me_n], own_sem.at[0]),
        pltpu.make_async_copy(rw_ref, rw_buf.at[me_l, me_n], own_sem.at[1]),
        pltpu.make_async_copy(grad_ref, coh.at[me_n], own_sem.at[2]),
    ]
    for copy in own_copies:
        copy.start()
    gate_copy = pltpu.make_async_copy(gate_ref, gate_buf, load_sem.at[0])
    up_copy = pltpu.make_async_copy(up_ref, up_buf, load_sem.at[1])
    gate_copy.start()
    up_copy.start()
    w_copies = [
        pltpu.make_async_copy(w_ref.at[cols(c), :], w_buf.at[cols(c), :], w_sem.at[c])
        for c in range(CHUNKS)
    ]
    pl.semaphore_wait(barrier, nodes + locals_ - 1)

    meta_copies, coh_copies = [], {}
    for k in range(1, nodes):
        meta_copies.append(remote(ids_ref, ids_buf.at[me_l, me_n], ids_send.at[k], ids_recv.at[k], node_at(k)))
        meta_copies.append(remote(rw_ref, rw_buf.at[me_l, me_n], rw_send.at[k], rw_recv.at[k], node_at(k)))
    for copy in meta_copies:
        copy.start()
    for c in range(CHUNKS):
        for k in range(1, nodes):
            copy = remote(
                grad_ref.at[:, cols(c)], coh.at[me_n, :, cols(c)],
                coh_send.at[c, k], coh_recv.at[c, k], node_at(k),
            )
            copy.start()
            coh_copies[c, k] = copy
    for copy in w_copies:
        copy.start()
    for copy in own_copies:
        copy.wait()
    for copy in meta_copies:
        copy.wait_recv()
    zmeta_copies = []
    for k in range(1, locals_):
        zmeta_copies.append(remote(ids_buf.at[me_l], ids_buf.at[me_l], zids_send.at[k], zids_recv.at[k], local_at(k)))
        zmeta_copies.append(remote(rw_buf.at[me_l], rw_buf.at[me_l], zrw_send.at[k], zrw_recv.at[k], local_at(k)))
    for copy in zmeta_copies:
        copy.start()

    own = ids_buf[me_l].astype(F32)
    own_ids = jnp.concatenate([own[n] for n in range(nodes)], axis=1)
    first = me_n * exp_group
    low = first.astype(F32)
    hits = [
        jnp.sum(jnp.where(own_ids == low + j, 1.0, 0.0), axis=0, keepdims=True)
        for j in range(exp_group)
    ]
    in_group = jnp.where(sum(hits) > 0, 1.0, 0.0)
    before = earlier_counts(stacked(hits + [in_group]), cohort)
    pick = one_hot(in_group, before[exp_group:exp_group + 1], group_tok).astype(BF16)

    def shifted(buf, copies_send, copies_recv, source, d, c, step):
        return remote(
            buf.at[source, :, cols(c)], buf.at[source, :, cols(c)],
            copies_send.at[d - 1, c], copies_recv.at[d - 1, c], {"local": me_l + step},
        )

    def right(source, d, c):
        return shifted(gath, right_send, right_recv, source, d, c, 1)

    def left(source, d, c):
        return shifted(gath, left_send, left_recv, source, d, c, -1)

    state = {}

    def prepare():
        for copy in zmeta_copies:
            copy.wait_recv()
        total = locals_ * cohort
        ids_all, rw_all = ids_buf[...].astype(F32), rw_buf[...].astype(F32)
        places = [(l, n) for l in range(locals_) for n in range(nodes)]
        all_ids = jnp.concatenate([ids_all[place] for place in places], axis=1)
        all_rw = jnp.concatenate([rw_all[place] for place in places], axis=1)
        match = jnp.where(all_ids == (first + me_l // owners).astype(F32), 1.0, 0.0)
        member = jnp.sum(match, axis=0, keepdims=True)
        row_weight = jnp.sum(match * all_rw, axis=0, keepdims=True)
        near = jnp.where((all_ids >= low) & (all_ids < low + exp_group), 1.0, 0.0)
        grouped = jnp.where(jnp.sum(near, axis=0, keepdims=True) > 0, 1.0, 0.0)
        earlier = earlier_counts(stacked([member, grouped]), cohort)
        which = (lax.broadcasted_iota(jnp.int32, (1, total), 1) // cohort).astype(F32)
        slot_hot = one_hot(member, earlier[0:1] + which * capacity, slots)
        pack_hot = one_hot(grouped, earlier[1:2] + which * group_tok, locals_ * group_tok)
        state["select"] = lax.dot_general(
            slot_hot.astype(BF16), pack_hot.astype(BF16),
            (((1,), (1,)), ((), ())), preferred_element_type=F32,
        ).astype(BF16)
        weight = jnp.sum(slot_hot * row_weight, axis=1, keepdims=True)
        state["weight"] = weight
        gate_copy.wait()
        up_copy.wait()
        gate = gate_buf[...].astype(F32)
        hidden = gate * jax.nn.sigmoid(gate) * up_buf[...].astype(F32)
        hidden_buf[...] = hidden
        wtd_out[0:slots, :] = (weight * hidden).astype(BF16)

    wtd_copy = remote(wtd_out.at[0:slots, :], wtd_out.at[slots:2 * slots, :], wtd_send, wtd_recv, peer)

    def cot_copy(c):
        part = pl.ds(c // 2 * cw, cw)
        return remote(
            peer_cot.at[:, part], cot_out.at[slots:2 * slots, part],
            cot_send.at[c // 2], cot_recv.at[c // 2], peer,
        )

    def finish(c):
        rows = gath[:, :, cols(c)].reshape(locals_ * group_tok, cw)
        cot = jnp.dot(state["select"], rows, preferred_element_type=F32).astype(BF16)
        part = pl.ds(c // 2 * cw, cw)

        @pl.when(me_r == c % 2)
        def _():
            cot_out[0:slots, part] = cot

        @pl.when(me_r != c % 2)
        def _():
            peer_cot[:, part] = cot

        w_copies[c].wait()
        term = jnp.dot(cot, w_buf[cols(c), :], preferred_element_type=F32)
        if c == 0:
            acc[...] = term
        else:
            acc[...] += term

        @pl.when(me_r != c % 2)
        def _():
            cot_copy(c).start()

    def outer(p):
        if p == 0:
            wtd_copy.wait_recv()
        cot_copy(2 * p).wait_recv()
        tile = cw // TILES
        for t in range(TILES):
            place = pl.ds(p * cw + t * tile, tile)
            down_out[place, :] = contract_rows(cot_out[:, place], wtd_out[...]).astype(BF16)

    for step in range(CHUNKS + locals_ - 1):
        if step < CHUNKS:
            for k in range(1, nodes):
                coh_copies[step, k].wait_recv()
            rows = coh[:, :, cols(step)].astype(F32).reshape(cohort, cw).astype(BF16)
            packed = jnp.dot(pick, rows, preferred_element_type=F32)
            gath[me_l, :, cols(step)] = packed.astype(BF16)

            @pl.when(me_l + 1 < locals_)
            def _():
                right(me_l, 1, step).start()

            @pl.when(me_l > 0)
            def _():
                left(me_l, 1, step).start()

        for d in range(1, locals_):
            c = step - d
            if not 0 <= c < CHUNKS:
                continue

            @pl.when(me_l >= d)
            def _():
                right(me_l - d, d, c).wait_recv()
                if d < locals_ - 1:
                    @pl.when(me_l + 1 < locals_)
                    def _():
                        right(me_l - d, d + 1, c).start()

            @pl.when(me_l + d < locals_)
            def _():
                left(me_l + d, d, c).wait_recv()
                if d < locals_ - 1:
                    @pl.when(me_l > 0)
                    def _():
                        left(me_l + d, d + 1, c).start()

        if step == locals_ - 2:
            prepare()
        if step >= locals_ - 1:
            done = step - locals_ + 1
            finish(done)
            if done == 0:
                wtd_copy.start()
            if done % 2 == 0 and done > 0:
                outer(done // 2 - 1)

    back = acc[...]
    shares = jnp.sum(hidden_buf[...] * back, axis=1, keepdims=True)
    share_buf[...] = jnp.broadcast_to(shares, (slots, 128)).astype(BF16).reshape(locals_, capacity, 128)
    back_buf[me_l] = share_buf[me_l]
    share_copies = [
        remote(share_buf.at[lax.rem(me_l + k, locals_)], back_buf.at[me_l], share_send.at[k], share_recv.at[k], local_at(k))
        for k in range(1, locals_)
    ]
    for copy in share_copies:
        copy.start()
    gate = gate_buf[...].astype(F32)
    sig = jax.nn.sigmoid(gate)
    scaled = state["weight"] * back
    ggate_out[...] = (scaled * up_buf[...].astype(F32) * sig * (1.0 + gate * (1.0 - sig))).astype(BF16)
    gup_out[...] = (scaled * gate * sig).astype(BF16)
    outer(half_chunks - 1)

    for copy in meta_copies + zmeta_copies + list(coh_copies.values()):
        copy.wait_send()
    for c in range(CHUNKS):
        @pl.when(me_l + 1 < locals_)
        def _():
            for d in range(locals_ - 1):
                @pl.when(me_l >= d)
                def _():
                    right(me_l - d, d + 1, c).wait_send()

        @pl.when(me_l > 0)
        def _():
            for d in range(locals_ - 1):
                @pl.when(me_l + d < locals_)
                def _():
                    left(me_l + d, d + 1, c).wait_send()
    wtd_copy.wait_send()
    for p in range(half_chunks):
        cot_copy(2 * p).wait_send()
    for copy in share_copies:
        copy.wait()
    route = []
    for j in range(exp_group):
        chosen = one_hot(hits[j], before[j:j + 1], capacity)
        value = jnp.zeros((capacity, 1), F32)
        for o in range(owners):
            value = value + back_buf[j * owners + o, :, 0:1].astype(F32)
        route.append(jnp.sum(chosen * value, axis=0, keepdims=True))
    route_out[...] = stacked(route)[0:exp_group].astype(BF16)


def write_kernel(gate_in, up_in, down_in, route_in, gate_to, up_to, down_to, route_to, sems, down_sems):
    rows = down_in.shape[0] // (2 * TILES)
    copies = [
        pltpu.make_async_copy(down_in.at[pl.ds(t * rows, rows)], down_to.at[pl.ds(t * rows, rows)], down_sems.at[t])
        for t in range(2 * TILES)
    ]
    pairs = ((gate_in, gate_to), (up_in, up_to), (route_in, route_to))
    copies += [pltpu.make_async_copy(src, dst, sems.at[t]) for t, (src, dst) in enumerate(pairs)]
    for copy in copies:
        copy.start()
    for copy in copies:
        copy.wait()


def gathered(nodes, locals_, group_tok, grad_out, expert_ids, route_weights, gate_pre, up_pre, w_down_t):
    tok, width = grad_out.shape
    top = expert_ids.shape[1]
    slots, hs = gate_pre.shape
    owners = H // hs
    exp_group = locals_ // owners
    cohort = nodes * tok
    capacity = slots // locals_
    half = width // 2
    dims = (nodes, locals_, tok, top, width, hs, group_tok, owners)
    dma = pltpu.SemaphoreType.DMA
    hbm = pl.BlockSpec(memory_space=pltpu.HBM)
    shapes = (
        jax.ShapeDtypeStruct((slots, hs), BF16),
        jax.ShapeDtypeStruct((slots, hs), BF16),
        jax.ShapeDtypeStruct((half, hs), BF16),
        jax.ShapeDtypeStruct((exp_group, cohort), BF16),
    )
    results = pl.pallas_call(
        functools.partial(routed_kernel, dims),
        out_shape=shapes,
        in_specs=[hbm] * 6,
        out_specs=tuple([pl.BlockSpec(memory_space=pltpu.VMEM)] * 4),
        scratch_shapes=[
            pltpu.VMEM((2 * slots, half), BF16),
            pltpu.VMEM((2 * slots, hs), BF16),
            pltpu.VMEM((locals_, nodes, top, tok), jnp.int32),
            pltpu.VMEM((locals_, nodes, top, tok), BF16),
            pltpu.VMEM((nodes, tok, width), BF16),
            pltpu.VMEM((locals_, group_tok, width), BF16),
            pltpu.VMEM((slots, half), BF16),
            pltpu.VMEM((width, hs), BF16),
            pltpu.VMEM((slots, hs), BF16),
            pltpu.VMEM((slots, hs), BF16),
            pltpu.VMEM((slots, hs), F32),
            pltpu.VMEM((slots, hs), F32),
            pltpu.VMEM((locals_, capacity, 128), BF16),
            pltpu.VMEM((locals_, capacity, 128), BF16),
            dma((2,)), dma((CHUNKS,)), dma((3,)),
            dma((nodes,)), dma((nodes,)), dma((nodes,)), dma((nodes,)),
            dma((CHUNKS, nodes)), dma((CHUNKS, nodes)),
            dma((locals_,)), dma((locals_,)), dma((locals_,)), dma((locals_,)),
            dma((locals_ - 1, CHUNKS)), dma((locals_ - 1, CHUNKS)),
            dma((locals_ - 1, CHUNKS)), dma((locals_ - 1, CHUNKS)),
            dma(()), dma(()), dma((CHUNKS // 2,)), dma((CHUNKS // 2,)),
            dma((locals_,)), dma((locals_,)),
        ],
        compiler_params=pltpu.CompilerParams(collective_id=0, has_side_effects=True, **KERNEL_PARAMS),
        name="routed",
    )(*[
        pltpu.with_memory_space_constraint(x, pltpu.HBM)
        for x in (expert_ids.T, route_weights.T, grad_out, gate_pre, up_pre, w_down_t)
    ])
    grad_gate, grad_up, grad_down, grad_route = pl.pallas_call(
        write_kernel,
        out_shape=shapes,
        in_specs=[pl.BlockSpec(memory_space=pl.ANY)] * 4,
        out_specs=tuple([pl.BlockSpec(memory_space=pl.ANY)] * 4),
        scratch_shapes=[dma((3,)), dma((2 * TILES,))],
        compiler_params=pltpu.CompilerParams(vmem_limit_bytes=1024 * 1024),
        name="write",
    )(*results)
    return grad_gate, grad_up, grad_down, grad_route.T


def swapped(block, axis, distance):
    count = lax.axis_size(axis)
    route = []
    for low in range(count):
        high = low | 1 << distance
        if high != low and high < count:
            route += [(low, high), (high, low)]
    return lax.ppermute(block, axis, route)


def outer_term(columns, weighted):
    return lax.dot_general(
        columns, weighted, (((0,), (0,)), ((), ())), preferred_element_type=jnp.float32
    )


def exchanged(grad_out, expert_ids, route_weights, gate_pre, up_pre, w_down_t):
    tok_dev, width = grad_out.shape
    slot_rows, hidden_slice = gate_pre.shape
    node_count = lax.axis_size("node")
    local_count = lax.axis_size("local")
    owners = H // hidden_slice
    exp_group = local_count // owners
    experts = exp_group * node_count
    capacity = slot_rows // local_count
    expert_range = lax.iota(jnp.int32, experts)
    route_hits = expert_ids[:, :, None] == expert_range[None, None, :]
    dense_weights = jnp.sum(
        jnp.where(route_hits, route_weights[:, :, None].astype(jnp.float32), 0.0), axis=1
    ).astype(jnp.bfloat16)
    cohort_grad, cohort_weights = (
        lax.all_gather(grad_out, "node", axis=0, tiled=True),
        lax.all_gather(dense_weights, "node", axis=0, tiled=True),
    )
    group_index = lax.axis_index("node")
    group_weights = lax.dynamic_slice_in_dim(cohort_weights, group_index * exp_group, exp_group, 1)
    routed = (group_weights != 0).astype(jnp.int32)
    earlier = jnp.cumsum(routed, axis=0) - routed
    slot_range = lax.iota(jnp.int32, capacity)
    select = (routed[:, :, None] == 1) & (earlier[:, :, None] == slot_range[None, None, :])
    select_half = select.astype(jnp.bfloat16)
    packed = jnp.einsum(
        "cjs,cd->jsd", select_half, cohort_grad, preferred_element_type=jnp.float32
    ).astype(jnp.bfloat16)
    packed_weights = jnp.einsum(
        "cjs,cj->js", select_half, group_weights, preferred_element_type=jnp.float32
    ).astype(jnp.bfloat16)
    send_grad = jnp.broadcast_to(packed[:, None], (exp_group, owners, capacity, width)).reshape(
        local_count, capacity, width
    )
    send_weights = jnp.broadcast_to(packed_weights[:, None], (exp_group, owners, capacity)).reshape(
        local_count, capacity
    )
    recv_grad, recv_weights = (
        lax.all_to_all(send_grad, "local", split_axis=0, concat_axis=0, tiled=True),
        lax.all_to_all(send_weights, "local", split_axis=0, concat_axis=0, tiled=True),
    )
    cotangent = recv_grad.reshape(slot_rows, width)
    weight = recv_weights.reshape(slot_rows, 1).astype(jnp.float32)
    gate_value = gate_pre.astype(jnp.float32)
    up_value = up_pre.astype(jnp.float32)
    backward = jnp.dot(cotangent, w_down_t, preferred_element_type=jnp.float32)
    sigmoid_gate = jax.nn.sigmoid(gate_value)
    activated = gate_value * sigmoid_gate
    hidden = activated * up_value
    shares = jnp.sum(hidden * backward, axis=1).astype(jnp.bfloat16)
    scaled = weight * backward
    grad_gate_pre = (
        scaled * up_value * sigmoid_gate * (1.0 + gate_value * (1.0 - sigmoid_gate))
    ).astype(jnp.bfloat16)
    grad_up_pre = (scaled * activated).astype(jnp.bfloat16)
    weighted = (weight * hidden).astype(jnp.bfloat16)
    returned = lax.all_to_all(
        shares.reshape(local_count, capacity), "local", split_axis=0, concat_axis=0, tiled=True
    )
    slice_sum = jnp.sum(returned.astype(jnp.float32).reshape(exp_group, owners, capacity), axis=1)
    grad_route = jnp.sum(jnp.where(select, slice_sum[None], 0.0), axis=2).astype(jnp.bfloat16)
    half_width = width // lax.axis_size("rep")
    replica = lax.axis_index("rep")
    own_cols = lax.dynamic_slice_in_dim(cotangent, replica * half_width, half_width, 1)
    peer_cols = lax.dynamic_slice_in_dim(cotangent, (1 - replica) * half_width, half_width, 1)
    got_cols, got_weighted = swapped((peer_cols, weighted), "rep", 0)
    own_term = outer_term(own_cols, weighted).astype(jnp.bfloat16).astype(jnp.float32)
    peer_term = outer_term(got_cols, got_weighted).astype(jnp.bfloat16).astype(jnp.float32)
    grad_down_t = (own_term + peer_term).astype(jnp.bfloat16)
    return (grad_gate_pre, grad_up_pre, grad_down_t, grad_route)


def per_device(grad_out, expert_ids, route_weights, gate_pre, up_pre, w_down_t):
    nodes, locals_ = lax.axis_size("node"), lax.axis_size("local")
    capacity = gate_pre.shape[0] // locals_
    group_tok = grad_out.shape[0] * expert_ids.shape[1] // PER_GROUP
    args = (grad_out, expert_ids, route_weights, gate_pre, up_pre, w_down_t)
    if group_tok > capacity:
        return exchanged(*args)
    return gathered(nodes, locals_, group_tok, *args)


def solution(mesh):
    placed = (
        P(("node", "local", "rep"), None),
        P(("node", "local", "rep"), None),
        P(("node", "local", "rep"), None),
        P("rep", ("node", "local")),
        P("rep", ("node", "local")),
        P(None, ("node", "local")),
    )
    return jax.shard_map(
        per_device,
        mesh=mesh,
        in_specs=placed,
        out_specs=(
            P("rep", ("node", "local")),
            P("rep", ("node", "local")),
            P("rep", ("node", "local")),
            P(("local", "rep"), "node"),
        ),
        check_vma=False,
    )
```

```python
import functools
import jax
import jax.numpy as jnp
from jax import lax
from jax.experimental import pallas as pl
from jax.experimental.pallas import tpu as pltpu
from jax.sharding import PartitionSpec as P

H = 1024
PER_GROUP = 2
CHUNKS = 4
TILES = 4
MESH = pl.DeviceIdType.MESH
F32 = jnp.float32
BF16 = jnp.bfloat16
KERNEL_PARAMS = dict(vmem_limit_bytes=40 * 1024 * 1024)


def contract_rows(left, right):
    return lax.dot_general(left, right, (((0,), (0,)), ((), ())), preferred_element_type=F32)


def one_hot(member, row, height):
    places = lax.broadcasted_iota(jnp.int32, (height, member.shape[1]), 0).astype(F32)
    return jnp.where((member > 0) & (row == places), 1.0, 0.0)


def earlier_counts(rows, block):
    count = rows.shape[1]
    above = lax.broadcasted_iota(jnp.int32, (count, count), 0)
    col = lax.broadcasted_iota(jnp.int32, (count, count), 1)
    strict = jnp.where((above < col) & (above // block == col // block), 1.0, 0.0).astype(BF16)
    return jnp.dot(rows.astype(BF16), strict, preferred_element_type=F32)


def stacked(rows):
    lines = lax.broadcasted_iota(jnp.int32, (8, rows[0].shape[1]), 0)
    out = jnp.zeros(lines.shape, F32)
    for place, row in enumerate(rows):
        out = jnp.where(lines == place, row, out)
    return out


def routed_kernel(
    dims, ids_ref, rw_ref, grad_ref, gate_ref, up_ref, w_ref,
    ggate_out, gup_out, down_out, route_out,
    cot_out, wtd_out, ids_buf, rw_buf, coh, gath, peer_cot, w_buf, gate_buf, up_buf, acc, hidden_buf, share_buf, back_buf,
    load_sem, w_sem, own_sem,
    ids_send, ids_recv, rw_send, rw_recv, coh_send, coh_recv,
    zids_send, zids_recv, zrw_send, zrw_recv,
    right_send, right_recv, left_send, left_recv,
    wtd_send, wtd_recv, cot_send, cot_recv, share_send, share_recv,
):
    nodes, locals_, tok, top, width, hs, group_tok, owners = dims
    cohort = nodes * tok
    exp_group = locals_ // owners
    slots = gate_ref.shape[0]
    capacity = slots // locals_
    half = width // 2
    cw = width // CHUNKS
    half_chunks = CHUNKS // 2
    me_n, me_l, me_r = lax.axis_index("node"), lax.axis_index("local"), lax.axis_index("rep")
    peer = {"rep": 1 - me_r}

    def node_at(k):
        return {"node": lax.rem(me_n + k, nodes)}

    def local_at(k):
        return {"local": lax.rem(me_l + k, locals_)}

    def remote(src, dst, send, recv, device):
        return pltpu.make_async_remote_copy(
            src_ref=src, dst_ref=dst, send_sem=send, recv_sem=recv,
            device_id=device, device_id_type=MESH,
        )

    barrier = pltpu.get_barrier_semaphore()
    for k in range(1, nodes):
        pl.semaphore_signal(barrier, inc=1, device_id=node_at(k), device_id_type=MESH)
    for k in range(1, locals_):
        pl.semaphore_signal(barrier, inc=1, device_id=local_at(k), device_id_type=MESH)
    pl.semaphore_signal(barrier, inc=1, device_id=peer, device_id_type=MESH)

    def cols(c):
        return pl.ds((c % 2) * half + (c // 2) * cw, cw)

    own_copies = [
        pltpu.make_async_copy(ids_ref, ids_buf.at[me_l, me_n], own_sem.at[0]),
        pltpu.make_async_copy(rw_ref, rw_buf.at[me_l, me_n], own_sem.at[1]),
        pltpu.make_async_copy(grad_ref, coh.at[me_n], own_sem.at[2]),
    ]
    for copy in own_copies:
        copy.start()
    gate_copy = pltpu.make_async_copy(gate_ref, gate_buf, load_sem.at[0])
    up_copy = pltpu.make_async_copy(up_ref, up_buf, load_sem.at[1])
    gate_copy.start()
    up_copy.start()
    w_copies = [
        pltpu.make_async_copy(w_ref.at[cols(c), :], w_buf.at[cols(c), :], w_sem.at[c])
        for c in range(CHUNKS)
    ]
    pl.semaphore_wait(barrier, nodes + locals_ - 1)

    meta_copies, coh_copies = [], {}
    for k in range(1, nodes):
        meta_copies.append(remote(ids_ref, ids_buf.at[me_l, me_n], ids_send.at[k], ids_recv.at[k], node_at(k)))
        meta_copies.append(remote(rw_ref, rw_buf.at[me_l, me_n], rw_send.at[k], rw_recv.at[k], node_at(k)))
    for copy in meta_copies:
        copy.start()
    for c in range(CHUNKS):
        for k in range(1, nodes):
            copy = remote(
                grad_ref.at[:, cols(c)], coh.at[me_n, :, cols(c)],
                coh_send.at[c, k], coh_recv.at[c, k], node_at(k),
            )
            copy.start()
            coh_copies[c, k] = copy
    for copy in w_copies:
        copy.start()
    for copy in own_copies:
        copy.wait()
    for copy in meta_copies:
        copy.wait_recv()
    zmeta_copies = []
    for k in range(1, locals_):
        zmeta_copies.append(remote(ids_buf.at[me_l], ids_buf.at[me_l], zids_send.at[k], zids_recv.at[k], local_at(k)))
        zmeta_copies.append(remote(rw_buf.at[me_l], rw_buf.at[me_l], zrw_send.at[k], zrw_recv.at[k], local_at(k)))
    for copy in zmeta_copies:
        copy.start()

    own = ids_buf[me_l].astype(F32)
    own_ids = jnp.concatenate([own[n] for n in range(nodes)], axis=1)
    first = me_n * exp_group
    low = first.astype(F32)
    hits = [
        jnp.sum(jnp.where(own_ids == low + j, 1.0, 0.0), axis=0, keepdims=True)
        for j in range(exp_group)
    ]
    in_group = jnp.where(sum(hits) > 0, 1.0, 0.0)
    before = earlier_counts(stacked(hits + [in_group]), cohort)
    pick = one_hot(in_group, before[exp_group:exp_group + 1], group_tok).astype(BF16)

    def shifted(buf, copies_send, copies_recv, source, d, c, step):
        return remote(
            buf.at[source, :, cols(c)], buf.at[source, :, cols(c)],
            copies_send.at[d - 1, c], copies_recv.at[d - 1, c], {"local": me_l + step},
        )

    def right(source, d, c):
        return shifted(gath, right_send, right_recv, source, d, c, 1)

    def left(source, d, c):
        return shifted(gath, left_send, left_recv, source, d, c, -1)

    state = {}

    def prepare():
        for copy in zmeta_copies:
            copy.wait_recv()
        total = locals_ * cohort
        ids_all, rw_all = ids_buf[...].astype(F32), rw_buf[...].astype(F32)
        places = [(l, n) for l in range(locals_) for n in range(nodes)]
        all_ids = jnp.concatenate([ids_all[place] for place in places], axis=1)
        all_rw = jnp.concatenate([rw_all[place] for place in places], axis=1)
        match = jnp.where(all_ids == (first + me_l // owners).astype(F32), 1.0, 0.0)
        member = jnp.sum(match, axis=0, keepdims=True)
        row_weight = jnp.sum(match * all_rw, axis=0, keepdims=True)
        near = jnp.where((all_ids >= low) & (all_ids < low + exp_group), 1.0, 0.0)
        grouped = jnp.where(jnp.sum(near, axis=0, keepdims=True) > 0, 1.0, 0.0)
        earlier = earlier_counts(stacked([member, grouped]), cohort)
        which = (lax.broadcasted_iota(jnp.int32, (1, total), 1) // cohort).astype(F32)
        slot_hot = one_hot(member, earlier[0:1] + which * capacity, slots)
        pack_hot = one_hot(grouped, earlier[1:2] + which * group_tok, locals_ * group_tok)
        state["select"] = lax.dot_general(
            slot_hot.astype(BF16), pack_hot.astype(BF16),
            (((1,), (1,)), ((), ())), preferred_element_type=F32,
        ).astype(BF16)
        weight = jnp.sum(slot_hot * row_weight, axis=1, keepdims=True)
        state["weight"] = weight
        gate_copy.wait()
        up_copy.wait()
        gate = gate_buf[...].astype(F32)
        hidden = gate * jax.nn.sigmoid(gate) * up_buf[...].astype(F32)
        hidden_buf[...] = hidden
        wtd_out[0:slots, :] = (weight * hidden).astype(BF16)

    wtd_copy = remote(wtd_out.at[0:slots, :], wtd_out.at[slots:2 * slots, :], wtd_send, wtd_recv, peer)

    def cot_copy(c):
        part = pl.ds(c // 2 * cw, cw)
        return remote(
            peer_cot.at[:, part], cot_out.at[slots:2 * slots, part],
            cot_send.at[c // 2], cot_recv.at[c // 2], peer,
        )

    def finish(c):
        rows = gath[:, :, cols(c)].reshape(locals_ * group_tok, cw)
        cot = jnp.dot(state["select"], rows, preferred_element_type=F32).astype(BF16)
        part = pl.ds(c // 2 * cw, cw)

        @pl.when(me_r == c % 2)
        def _():
            cot_out[0:slots, part] = cot

        @pl.when(me_r != c % 2)
        def _():
            peer_cot[:, part] = cot

        w_copies[c].wait()
        term = jnp.dot(cot, w_buf[cols(c), :], preferred_element_type=F32)
        if c == 0:
            acc[...] = term
        else:
            acc[...] += term

        @pl.when(me_r != c % 2)
        def _():
            cot_copy(c).start()

    def outer(p):
        if p == 0:
            wtd_copy.wait_recv()
        cot_copy(2 * p).wait_recv()
        tile = cw // TILES
        for t in range(TILES):
            place = pl.ds(p * cw + t * tile, tile)
            down_out[place, :] = contract_rows(cot_out[:, place], wtd_out[...]).astype(BF16)

    def send_own(c):
        for k in range(1, nodes):
            coh_copies[c, k].wait_recv()
        rows = coh[:, :, cols(c)].astype(F32).reshape(cohort, cw).astype(BF16)
        packed = jnp.dot(pick, rows, preferred_element_type=F32)
        gath[me_l, :, cols(c)] = packed.astype(BF16)

        @pl.when(me_l + 1 < locals_)
        def _():
            right(me_l, 1, c).start()

        @pl.when(me_l > 0)
        def _():
            left(me_l, 1, c).start()

    def relay(d, c):
        @pl.when(me_l >= d)
        def _():
            right(me_l - d, d, c).wait_recv()
            if d < locals_ - 1:
                @pl.when(me_l + 1 < locals_)
                def _():
                    right(me_l - d, d + 1, c).start()

        @pl.when(me_l + d < locals_)
        def _():
            left(me_l + d, d, c).wait_recv()
            if d < locals_ - 1:
                @pl.when(me_l > 0)
                def _():
                    left(me_l + d, d + 1, c).start()

    for c in range(CHUNKS):
        send_own(c)
    for d in range(1, locals_):
        if d == locals_ - 1:
            prepare()
        for c in range(CHUNKS):
            relay(d, c)
            if d == locals_ - 1:
                finish(c)
                if c == 0:
                    wtd_copy.start()
                if c % 2 == 0 and c > 0:
                    outer(c // 2 - 1)

    back = acc[...]
    shares = jnp.sum(hidden_buf[...] * back, axis=1, keepdims=True)
    share_buf[...] = jnp.broadcast_to(shares, (slots, 128)).astype(BF16).reshape(locals_, capacity, 128)
    back_buf[me_l] = share_buf[me_l]
    share_copies = [
        remote(share_buf.at[lax.rem(me_l + k, locals_)], back_buf.at[me_l], share_send.at[k], share_recv.at[k], local_at(k))
        for k in range(1, locals_)
    ]
    for copy in share_copies:
        copy.start()
    gate = gate_buf[...].astype(F32)
    sig = jax.nn.sigmoid(gate)
    scaled = state["weight"] * back
    ggate_out[...] = (scaled * up_buf[...].astype(F32) * sig * (1.0 + gate * (1.0 - sig))).astype(BF16)
    gup_out[...] = (scaled * gate * sig).astype(BF16)
    outer(half_chunks - 1)

    for copy in meta_copies + zmeta_copies + list(coh_copies.values()):
        copy.wait_send()
    for c in range(CHUNKS):
        @pl.when(me_l + 1 < locals_)
        def _():
            for d in range(locals_ - 1):
                @pl.when(me_l >= d)
                def _():
                    right(me_l - d, d + 1, c).wait_send()

        @pl.when(me_l > 0)
        def _():
            for d in range(locals_ - 1):
                @pl.when(me_l + d < locals_)
                def _():
                    left(me_l + d, d + 1, c).wait_send()
    wtd_copy.wait_send()
    for p in range(half_chunks):
        cot_copy(2 * p).wait_send()
    for copy in share_copies:
        copy.wait()
    route = []
    for j in range(exp_group):
        chosen = one_hot(hits[j], before[j:j + 1], capacity)
        value = jnp.zeros((capacity, 1), F32)
        for o in range(owners):
            value = value + back_buf[j * owners + o, :, 0:1].astype(F32)
        route.append(jnp.sum(chosen * value, axis=0, keepdims=True))
    route_out[...] = stacked(route)[0:exp_group].astype(BF16)


def write_kernel(gate_in, up_in, down_in, route_in, gate_to, up_to, down_to, route_to, sems, down_sems):
    rows = down_in.shape[0] // (2 * TILES)
    copies = [
        pltpu.make_async_copy(down_in.at[pl.ds(t * rows, rows)], down_to.at[pl.ds(t * rows, rows)], down_sems.at[t])
        for t in range(2 * TILES)
    ]
    pairs = ((gate_in, gate_to), (up_in, up_to), (route_in, route_to))
    copies += [pltpu.make_async_copy(src, dst, sems.at[t]) for t, (src, dst) in enumerate(pairs)]
    for copy in copies:
        copy.start()
    for copy in copies:
        copy.wait()


def gathered(nodes, locals_, group_tok, grad_out, expert_ids, route_weights, gate_pre, up_pre, w_down_t):
    tok, width = grad_out.shape
    top = expert_ids.shape[1]
    slots, hs = gate_pre.shape
    owners = H // hs
    exp_group = locals_ // owners
    cohort = nodes * tok
    capacity = slots // locals_
    half = width // 2
    dims = (nodes, locals_, tok, top, width, hs, group_tok, owners)
    dma = pltpu.SemaphoreType.DMA
    hbm = pl.BlockSpec(memory_space=pltpu.HBM)
    shapes = (
        jax.ShapeDtypeStruct((slots, hs), BF16),
        jax.ShapeDtypeStruct((slots, hs), BF16),
        jax.ShapeDtypeStruct((half, hs), BF16),
        jax.ShapeDtypeStruct((exp_group, cohort), BF16),
    )
    results = pl.pallas_call(
        functools.partial(routed_kernel, dims),
        out_shape=shapes,
        in_specs=[hbm] * 6,
        out_specs=tuple([pl.BlockSpec(memory_space=pltpu.VMEM)] * 4),
        scratch_shapes=[
            pltpu.VMEM((2 * slots, half), BF16),
            pltpu.VMEM((2 * slots, hs), BF16),
            pltpu.VMEM((locals_, nodes, top, tok), jnp.int32),
            pltpu.VMEM((locals_, nodes, top, tok), BF16),
            pltpu.VMEM((nodes, tok, width), BF16),
            pltpu.VMEM((locals_, group_tok, width), BF16),
            pltpu.VMEM((slots, half), BF16),
            pltpu.VMEM((width, hs), BF16),
            pltpu.VMEM((slots, hs), BF16),
            pltpu.VMEM((slots, hs), BF16),
            pltpu.VMEM((slots, hs), F32),
            pltpu.VMEM((slots, hs), F32),
            pltpu.VMEM((locals_, capacity, 128), BF16),
            pltpu.VMEM((locals_, capacity, 128), BF16),
            dma((2,)), dma((CHUNKS,)), dma((3,)),
            dma((nodes,)), dma((nodes,)), dma((nodes,)), dma((nodes,)),
            dma((CHUNKS, nodes)), dma((CHUNKS, nodes)),
            dma((locals_,)), dma((locals_,)), dma((locals_,)), dma((locals_,)),
            dma((locals_ - 1, CHUNKS)), dma((locals_ - 1, CHUNKS)),
            dma((locals_ - 1, CHUNKS)), dma((locals_ - 1, CHUNKS)),
            dma(()), dma(()), dma((CHUNKS // 2,)), dma((CHUNKS // 2,)),
            dma((locals_,)), dma((locals_,)),
        ],
        compiler_params=pltpu.CompilerParams(collective_id=0, has_side_effects=True, **KERNEL_PARAMS),
        name="routed",
    )(*[
        pltpu.with_memory_space_constraint(x, pltpu.HBM)
        for x in (expert_ids.T, route_weights.T, grad_out, gate_pre, up_pre, w_down_t)
    ])
    grad_gate, grad_up, grad_down, grad_route = pl.pallas_call(
        write_kernel,
        out_shape=shapes,
        in_specs=[pl.BlockSpec(memory_space=pl.ANY)] * 4,
        out_specs=tuple([pl.BlockSpec(memory_space=pl.ANY)] * 4),
        scratch_shapes=[dma((3,)), dma((2 * TILES,))],
        compiler_params=pltpu.CompilerParams(vmem_limit_bytes=1024 * 1024),
        name="write",
    )(*results)
    return grad_gate, grad_up, grad_down, grad_route.T


def swapped(block, axis, distance):
    count = lax.axis_size(axis)
    route = []
    for low in range(count):
        high = low | 1 << distance
        if high != low and high < count:
            route += [(low, high), (high, low)]
    return lax.ppermute(block, axis, route)


def outer_term(columns, weighted):
    return lax.dot_general(
        columns, weighted, (((0,), (0,)), ((), ())), preferred_element_type=jnp.float32
    )


def exchanged(grad_out, expert_ids, route_weights, gate_pre, up_pre, w_down_t):
    tok_dev, width = grad_out.shape
    slot_rows, hidden_slice = gate_pre.shape
    node_count = lax.axis_size("node")
    local_count = lax.axis_size("local")
    owners = H // hidden_slice
    exp_group = local_count // owners
    experts = exp_group * node_count
    capacity = slot_rows // local_count
    expert_range = lax.iota(jnp.int32, experts)
    route_hits = expert_ids[:, :, None] == expert_range[None, None, :]
    dense_weights = jnp.sum(
        jnp.where(route_hits, route_weights[:, :, None].astype(jnp.float32), 0.0), axis=1
    ).astype(jnp.bfloat16)
    cohort_grad, cohort_weights = (
        lax.all_gather(grad_out, "node", axis=0, tiled=True),
        lax.all_gather(dense_weights, "node", axis=0, tiled=True),
    )
    group_index = lax.axis_index("node")
    group_weights = lax.dynamic_slice_in_dim(cohort_weights, group_index * exp_group, exp_group, 1)
    routed = (group_weights != 0).astype(jnp.int32)
    earlier = jnp.cumsum(routed, axis=0) - routed
    slot_range = lax.iota(jnp.int32, capacity)
    select = (routed[:, :, None] == 1) & (earlier[:, :, None] == slot_range[None, None, :])
    select_half = select.astype(jnp.bfloat16)
    packed = jnp.einsum(
        "cjs,cd->jsd", select_half, cohort_grad, preferred_element_type=jnp.float32
    ).astype(jnp.bfloat16)
    packed_weights = jnp.einsum(
        "cjs,cj->js", select_half, group_weights, preferred_element_type=jnp.float32
    ).astype(jnp.bfloat16)
    send_grad = jnp.broadcast_to(packed[:, None], (exp_group, owners, capacity, width)).reshape(
        local_count, capacity, width
    )
    send_weights = jnp.broadcast_to(packed_weights[:, None], (exp_group, owners, capacity)).reshape(
        local_count, capacity
    )
    recv_grad, recv_weights = (
        lax.all_to_all(send_grad, "local", split_axis=0, concat_axis=0, tiled=True),
        lax.all_to_all(send_weights, "local", split_axis=0, concat_axis=0, tiled=True),
    )
    cotangent = recv_grad.reshape(slot_rows, width)
    weight = recv_weights.reshape(slot_rows, 1).astype(jnp.float32)
    gate_value = gate_pre.astype(jnp.float32)
    up_value = up_pre.astype(jnp.float32)
    backward = jnp.dot(cotangent, w_down_t, preferred_element_type=jnp.float32)
    sigmoid_gate = jax.nn.sigmoid(gate_value)
    activated = gate_value * sigmoid_gate
    hidden = activated * up_value
    shares = jnp.sum(hidden * backward, axis=1).astype(jnp.bfloat16)
    scaled = weight * backward
    grad_gate_pre = (
        scaled * up_value * sigmoid_gate * (1.0 + gate_value * (1.0 - sigmoid_gate))
    ).astype(jnp.bfloat16)
    grad_up_pre = (scaled * activated).astype(jnp.bfloat16)
    weighted = (weight * hidden).astype(jnp.bfloat16)
    returned = lax.all_to_all(
        shares.reshape(local_count, capacity), "local", split_axis=0, concat_axis=0, tiled=True
    )
    slice_sum = jnp.sum(returned.astype(jnp.float32).reshape(exp_group, owners, capacity), axis=1)
    grad_route = jnp.sum(jnp.where(select, slice_sum[None], 0.0), axis=2).astype(jnp.bfloat16)
    half_width = width // lax.axis_size("rep")
    replica = lax.axis_index("rep")
    own_cols = lax.dynamic_slice_in_dim(cotangent, replica * half_width, half_width, 1)
    peer_cols = lax.dynamic_slice_in_dim(cotangent, (1 - replica) * half_width, half_width, 1)
    got_cols, got_weighted = swapped((peer_cols, weighted), "rep", 0)
    own_term = outer_term(own_cols, weighted).astype(jnp.bfloat16).astype(jnp.float32)
    peer_term = outer_term(got_cols, got_weighted).astype(jnp.bfloat16).astype(jnp.float32)
    grad_down_t = (own_term + peer_term).astype(jnp.bfloat16)
    return (grad_gate_pre, grad_up_pre, grad_down_t, grad_route)


def per_device(grad_out, expert_ids, route_weights, gate_pre, up_pre, w_down_t):
    nodes, locals_ = lax.axis_size("node"), lax.axis_size("local")
    capacity = gate_pre.shape[0] // locals_
    group_tok = grad_out.shape[0] * expert_ids.shape[1] // PER_GROUP
    args = (grad_out, expert_ids, route_weights, gate_pre, up_pre, w_down_t)
    if group_tok > capacity:
        return exchanged(*args)
    return gathered(nodes, locals_, group_tok, *args)


def solution(mesh):
    placed = (
        P(("node", "local", "rep"), None),
        P(("node", "local", "rep"), None),
        P(("node", "local", "rep"), None),
        P("rep", ("node", "local")),
        P("rep", ("node", "local")),
        P(None, ("node", "local")),
    )
    return jax.shard_map(
        per_device,
        mesh=mesh,
        in_specs=placed,
        out_specs=(
            P("rep", ("node", "local")),
            P("rep", ("node", "local")),
            P("rep", ("node", "local")),
            P(("local", "rep"), "node"),
        ),
        check_vma=False,
    )
```

```python
import functools
import jax
import jax.numpy as jnp
from jax import lax
from jax.experimental import pallas as pl
from jax.experimental.pallas import tpu as pltpu
from jax.sharding import PartitionSpec as P

H = 1024
PER_GROUP = 2
CHUNKS = 4
TILES = 4
MESH = pl.DeviceIdType.MESH
F32 = jnp.float32
BF16 = jnp.bfloat16
KERNEL_PARAMS = dict(vmem_limit_bytes=40 * 1024 * 1024)


def contract_rows(left, right):
    return lax.dot_general(left, right, (((0,), (0,)), ((), ())), preferred_element_type=F32)


def one_hot(member, row, height):
    places = lax.broadcasted_iota(jnp.int32, (height, member.shape[1]), 0).astype(F32)
    return jnp.where((member > 0) & (row == places), 1.0, 0.0)


def earlier_counts(rows, block):
    count = rows.shape[1]
    above = lax.broadcasted_iota(jnp.int32, (count, count), 0)
    col = lax.broadcasted_iota(jnp.int32, (count, count), 1)
    strict = jnp.where((above < col) & (above // block == col // block), 1.0, 0.0).astype(BF16)
    return jnp.dot(rows.astype(BF16), strict, preferred_element_type=F32)


def stacked(rows):
    lines = lax.broadcasted_iota(jnp.int32, (8, rows[0].shape[1]), 0)
    out = jnp.zeros(lines.shape, F32)
    for place, row in enumerate(rows):
        out = jnp.where(lines == place, row, out)
    return out


def routed_kernel(
    dims, ids_ref, rw_ref, grad_ref, gate_ref, up_ref, w_ref,
    ggate_out, gup_out, down_out, route_out,
    cot_out, wtd_out, ids_buf, rw_buf, coh, gath, peer_cot, w_buf, gate_buf, up_buf, acc, hidden_buf, share_buf, back_buf,
    load_sem, w_sem, own_sem,
    ids_send, ids_recv, rw_send, rw_recv, coh_send, coh_recv,
    zids_send, zids_recv, zrw_send, zrw_recv,
    right_send, right_recv, left_send, left_recv,
    wtd_send, wtd_recv, cot_send, cot_recv, share_send, share_recv,
):
    nodes, locals_, tok, top, width, hs, group_tok, owners = dims
    cohort = nodes * tok
    exp_group = locals_ // owners
    slots = gate_ref.shape[0]
    capacity = slots // locals_
    half = width // 2
    cw = width // CHUNKS
    half_chunks = CHUNKS // 2
    me_n, me_l, me_r = lax.axis_index("node"), lax.axis_index("local"), lax.axis_index("rep")
    peer = {"rep": 1 - me_r}

    def node_at(k):
        return {"node": lax.rem(me_n + k, nodes)}

    def local_at(k):
        return {"local": lax.rem(me_l + k, locals_)}

    def remote(src, dst, send, recv, device):
        return pltpu.make_async_remote_copy(
            src_ref=src, dst_ref=dst, send_sem=send, recv_sem=recv,
            device_id=device, device_id_type=MESH,
        )

    barrier = pltpu.get_barrier_semaphore()
    for k in range(1, nodes):
        pl.semaphore_signal(barrier, inc=1, device_id=node_at(k), device_id_type=MESH)
    for k in range(1, locals_):
        pl.semaphore_signal(barrier, inc=1, device_id=local_at(k), device_id_type=MESH)
    pl.semaphore_signal(barrier, inc=1, device_id=peer, device_id_type=MESH)

    def cols(c):
        return pl.ds((c % 2) * half + (c // 2) * cw, cw)

    own_copies = [
        pltpu.make_async_copy(ids_ref, ids_buf.at[me_l, me_n], own_sem.at[0]),
        pltpu.make_async_copy(rw_ref, rw_buf.at[me_l, me_n], own_sem.at[1]),
        pltpu.make_async_copy(grad_ref, coh.at[me_n], own_sem.at[2]),
    ]
    for copy in own_copies:
        copy.start()
    gate_copy = pltpu.make_async_copy(gate_ref, gate_buf, load_sem.at[0])
    up_copy = pltpu.make_async_copy(up_ref, up_buf, load_sem.at[1])
    gate_copy.start()
    up_copy.start()
    w_copies = [
        pltpu.make_async_copy(w_ref.at[cols(c), :], w_buf.at[cols(c), :], w_sem.at[c])
        for c in range(CHUNKS)
    ]
    pl.semaphore_wait(barrier, nodes + locals_ - 1)

    meta_copies, coh_copies = [], {}
    for k in range(1, nodes):
        meta_copies.append(remote(ids_ref, ids_buf.at[me_l, me_n], ids_send.at[k], ids_recv.at[k], node_at(k)))
        meta_copies.append(remote(rw_ref, rw_buf.at[me_l, me_n], rw_send.at[k], rw_recv.at[k], node_at(k)))
    for copy in meta_copies:
        copy.start()
    for c in range(CHUNKS):
        for k in range(1, nodes):
            copy = remote(
                grad_ref.at[:, cols(c)], coh.at[me_n, :, cols(c)],
                coh_send.at[c, k], coh_recv.at[c, k], node_at(k),
            )
            copy.start()
            coh_copies[c, k] = copy
    for copy in w_copies:
        copy.start()
    for copy in own_copies:
        copy.wait()
    for copy in meta_copies:
        copy.wait_recv()
    zmeta_copies = []
    for k in range(1, locals_):
        zmeta_copies.append(remote(ids_buf.at[me_l], ids_buf.at[me_l], zids_send.at[k], zids_recv.at[k], local_at(k)))
        zmeta_copies.append(remote(rw_buf.at[me_l], rw_buf.at[me_l], zrw_send.at[k], zrw_recv.at[k], local_at(k)))
    for copy in zmeta_copies:
        copy.start()

    own = ids_buf[me_l].astype(F32)
    own_ids = jnp.concatenate([own[n] for n in range(nodes)], axis=1)
    first = me_n * exp_group
    low = first.astype(F32)
    hits = [
        jnp.sum(jnp.where(own_ids == low + j, 1.0, 0.0), axis=0, keepdims=True)
        for j in range(exp_group)
    ]
    in_group = jnp.where(sum(hits) > 0, 1.0, 0.0)
    before = earlier_counts(stacked(hits + [in_group]), cohort)
    pick = one_hot(in_group, before[exp_group:exp_group + 1], group_tok).astype(BF16)

    def shifted(buf, copies_send, copies_recv, source, d, c, step):
        return remote(
            buf.at[source, :, cols(c)], buf.at[source, :, cols(c)],
            copies_send.at[d - 1, c], copies_recv.at[d - 1, c], {"local": me_l + step},
        )

    def right(source, d, c):
        return shifted(gath, right_send, right_recv, source, d, c, 1)

    def left(source, d, c):
        return shifted(gath, left_send, left_recv, source, d, c, -1)

    state = {}

    def prepare():
        for copy in zmeta_copies:
            copy.wait_recv()
        total = locals_ * cohort
        ids_all, rw_all = ids_buf[...].astype(F32), rw_buf[...].astype(F32)
        places = [(l, n) for l in range(locals_) for n in range(nodes)]
        all_ids = jnp.concatenate([ids_all[place] for place in places], axis=1)
        all_rw = jnp.concatenate([rw_all[place] for place in places], axis=1)
        match = jnp.where(all_ids == (first + me_l // owners).astype(F32), 1.0, 0.0)
        member = jnp.sum(match, axis=0, keepdims=True)
        row_weight = jnp.sum(match * all_rw, axis=0, keepdims=True)
        near = jnp.where((all_ids >= low) & (all_ids < low + exp_group), 1.0, 0.0)
        grouped = jnp.where(jnp.sum(near, axis=0, keepdims=True) > 0, 1.0, 0.0)
        earlier = earlier_counts(stacked([member, grouped]), cohort)
        which = (lax.broadcasted_iota(jnp.int32, (1, total), 1) // cohort).astype(F32)
        slot_hot = one_hot(member, earlier[0:1] + which * capacity, slots)
        pack_hot = one_hot(grouped, earlier[1:2] + which * group_tok, locals_ * group_tok)
        state["select"] = lax.dot_general(
            slot_hot.astype(BF16), pack_hot.astype(BF16),
            (((1,), (1,)), ((), ())), preferred_element_type=F32,
        ).astype(BF16)
        weight = jnp.sum(slot_hot * row_weight, axis=1, keepdims=True)
        state["weight"] = weight
        gate_copy.wait()
        up_copy.wait()
        gate = gate_buf[...].astype(F32)
        hidden = gate * jax.nn.sigmoid(gate) * up_buf[...].astype(F32)
        hidden_buf[...] = hidden
        wtd_out[0:slots, :] = (weight * hidden).astype(BF16)

    wtd_copy = remote(wtd_out.at[0:slots, :], wtd_out.at[slots:2 * slots, :], wtd_send, wtd_recv, peer)

    def cot_copy(c):
        part = pl.ds(c // 2 * cw, cw)
        return remote(
            peer_cot.at[:, part], cot_out.at[slots:2 * slots, part],
            cot_send.at[c // 2], cot_recv.at[c // 2], peer,
        )

    def finish(c):
        rows = gath[:, :, cols(c)].reshape(locals_ * group_tok, cw)
        cot = jnp.dot(state["select"], rows, preferred_element_type=F32).astype(BF16)
        part = pl.ds(c // 2 * cw, cw)

        @pl.when(me_r == c % 2)
        def _():
            cot_out[0:slots, part] = cot

        @pl.when(me_r != c % 2)
        def _():
            peer_cot[:, part] = cot

        w_copies[c].wait()
        term = jnp.dot(cot, w_buf[cols(c), :], preferred_element_type=F32)
        if c == 0:
            acc[...] = term
        else:
            acc[...] += term

        @pl.when(me_r != c % 2)
        def _():
            cot_copy(c).start()

    def outer(p):
        if p == 0:
            wtd_copy.wait_recv()
        cot_copy(2 * p).wait_recv()
        tile = cw // TILES
        for t in range(TILES):
            place = pl.ds(p * cw + t * tile, tile)
            down_out[place, :] = contract_rows(cot_out[:, place], wtd_out[...]).astype(BF16)

    def send_own(c):
        for k in range(1, nodes):
            coh_copies[c, k].wait_recv()
        rows = coh[:, :, cols(c)].astype(F32).reshape(cohort, cw).astype(BF16)
        packed = jnp.dot(pick, rows, preferred_element_type=F32)
        gath[me_l, :, cols(c)] = packed.astype(BF16)

        @pl.when(me_l + 1 < locals_)
        def _():
            right(me_l, 1, c).start()

        @pl.when(me_l > 0)
        def _():
            left(me_l, 1, c).start()

    def relay(d, c):
        @pl.when(me_l >= d)
        def _():
            right(me_l - d, d, c).wait_recv()
            if d < locals_ - 1:
                @pl.when(me_l + 1 < locals_)
                def _():
                    right(me_l - d, d + 1, c).start()

        @pl.when(me_l + d < locals_)
        def _():
            left(me_l + d, d, c).wait_recv()
            if d < locals_ - 1:
                @pl.when(me_l > 0)
                def _():
                    left(me_l + d, d + 1, c).start()

    for c in range(CHUNKS):
        send_own(c)
    for d in range(1, locals_):
        if d == locals_ - 1:
            prepare()
        for c in range(CHUNKS):
            relay(d, c)
            if d == locals_ - 1:
                finish(c)
                if c == 0:
                    wtd_copy.start()

    back = acc[...]
    shares = jnp.sum(hidden_buf[...] * back, axis=1, keepdims=True)
    share_buf[...] = jnp.broadcast_to(shares, (slots, 128)).astype(BF16).reshape(locals_, capacity, 128)
    back_buf[me_l] = share_buf[me_l]
    share_copies = [
        remote(share_buf.at[lax.rem(me_l + k, locals_)], back_buf.at[me_l], share_send.at[k], share_recv.at[k], local_at(k))
        for k in range(1, locals_)
    ]
    for copy in share_copies:
        copy.start()
    gate = gate_buf[...].astype(F32)
    sig = jax.nn.sigmoid(gate)
    scaled = state["weight"] * back
    ggate_out[...] = (scaled * up_buf[...].astype(F32) * sig * (1.0 + gate * (1.0 - sig))).astype(BF16)
    gup_out[...] = (scaled * gate * sig).astype(BF16)
    for p in range(half_chunks):
        outer(p)

    for copy in meta_copies + zmeta_copies + list(coh_copies.values()):
        copy.wait_send()
    for c in range(CHUNKS):
        @pl.when(me_l + 1 < locals_)
        def _():
            for d in range(locals_ - 1):
                @pl.when(me_l >= d)
                def _():
                    right(me_l - d, d + 1, c).wait_send()

        @pl.when(me_l > 0)
        def _():
            for d in range(locals_ - 1):
                @pl.when(me_l + d < locals_)
                def _():
                    left(me_l + d, d + 1, c).wait_send()
    wtd_copy.wait_send()
    for p in range(half_chunks):
        cot_copy(2 * p).wait_send()
    for copy in share_copies:
        copy.wait()
    route = []
    for j in range(exp_group):
        chosen = one_hot(hits[j], before[j:j + 1], capacity)
        value = jnp.zeros((capacity, 1), F32)
        for o in range(owners):
            value = value + back_buf[j * owners + o, :, 0:1].astype(F32)
        route.append(jnp.sum(chosen * value, axis=0, keepdims=True))
    route_out[...] = stacked(route)[0:exp_group].astype(BF16)


def write_kernel(gate_in, up_in, down_in, route_in, gate_to, up_to, down_to, route_to, sems, down_sems):
    rows = down_in.shape[0] // (2 * TILES)
    copies = [
        pltpu.make_async_copy(down_in.at[pl.ds(t * rows, rows)], down_to.at[pl.ds(t * rows, rows)], down_sems.at[t])
        for t in range(2 * TILES)
    ]
    pairs = ((gate_in, gate_to), (up_in, up_to), (route_in, route_to))
    copies += [pltpu.make_async_copy(src, dst, sems.at[t]) for t, (src, dst) in enumerate(pairs)]
    for copy in copies:
        copy.start()
    for copy in copies:
        copy.wait()


def gathered(nodes, locals_, group_tok, grad_out, expert_ids, route_weights, gate_pre, up_pre, w_down_t):
    tok, width = grad_out.shape
    top = expert_ids.shape[1]
    slots, hs = gate_pre.shape
    owners = H // hs
    exp_group = locals_ // owners
    cohort = nodes * tok
    capacity = slots // locals_
    half = width // 2
    dims = (nodes, locals_, tok, top, width, hs, group_tok, owners)
    dma = pltpu.SemaphoreType.DMA
    hbm = pl.BlockSpec(memory_space=pltpu.HBM)
    shapes = (
        jax.ShapeDtypeStruct((slots, hs), BF16),
        jax.ShapeDtypeStruct((slots, hs), BF16),
        jax.ShapeDtypeStruct((half, hs), BF16),
        jax.ShapeDtypeStruct((exp_group, cohort), BF16),
    )
    results = pl.pallas_call(
        functools.partial(routed_kernel, dims),
        out_shape=shapes,
        in_specs=[hbm] * 6,
        out_specs=tuple([pl.BlockSpec(memory_space=pltpu.VMEM)] * 4),
        scratch_shapes=[
            pltpu.VMEM((2 * slots, half), BF16),
            pltpu.VMEM((2 * slots, hs), BF16),
            pltpu.VMEM((locals_, nodes, top, tok), jnp.int32),
            pltpu.VMEM((locals_, nodes, top, tok), BF16),
            pltpu.VMEM((nodes, tok, width), BF16),
            pltpu.VMEM((locals_, group_tok, width), BF16),
            pltpu.VMEM((slots, half), BF16),
            pltpu.VMEM((width, hs), BF16),
            pltpu.VMEM((slots, hs), BF16),
            pltpu.VMEM((slots, hs), BF16),
            pltpu.VMEM((slots, hs), F32),
            pltpu.VMEM((slots, hs), F32),
            pltpu.VMEM((locals_, capacity, 128), BF16),
            pltpu.VMEM((locals_, capacity, 128), BF16),
            dma((2,)), dma((CHUNKS,)), dma((3,)),
            dma((nodes,)), dma((nodes,)), dma((nodes,)), dma((nodes,)),
            dma((CHUNKS, nodes)), dma((CHUNKS, nodes)),
            dma((locals_,)), dma((locals_,)), dma((locals_,)), dma((locals_,)),
            dma((locals_ - 1, CHUNKS)), dma((locals_ - 1, CHUNKS)),
            dma((locals_ - 1, CHUNKS)), dma((locals_ - 1, CHUNKS)),
            dma(()), dma(()), dma((CHUNKS // 2,)), dma((CHUNKS // 2,)),
            dma((locals_,)), dma((locals_,)),
        ],
        compiler_params=pltpu.CompilerParams(collective_id=0, has_side_effects=True, **KERNEL_PARAMS),
        name="routed",
    )(*[
        pltpu.with_memory_space_constraint(x, pltpu.HBM)
        for x in (expert_ids.T, route_weights.T, grad_out, gate_pre, up_pre, w_down_t)
    ])
    grad_gate, grad_up, grad_down, grad_route = pl.pallas_call(
        write_kernel,
        out_shape=shapes,
        in_specs=[pl.BlockSpec(memory_space=pl.ANY)] * 4,
        out_specs=tuple([pl.BlockSpec(memory_space=pl.ANY)] * 4),
        scratch_shapes=[dma((3,)), dma((2 * TILES,))],
        compiler_params=pltpu.CompilerParams(vmem_limit_bytes=1024 * 1024),
        name="write",
    )(*results)
    return grad_gate, grad_up, grad_down, grad_route.T


def swapped(block, axis, distance):
    count = lax.axis_size(axis)
    route = []
    for low in range(count):
        high = low | 1 << distance
        if high != low and high < count:
            route += [(low, high), (high, low)]
    return lax.ppermute(block, axis, route)


def outer_term(columns, weighted):
    return lax.dot_general(
        columns, weighted, (((0,), (0,)), ((), ())), preferred_element_type=jnp.float32
    )


def exchanged(grad_out, expert_ids, route_weights, gate_pre, up_pre, w_down_t):
    tok_dev, width = grad_out.shape
    slot_rows, hidden_slice = gate_pre.shape
    node_count = lax.axis_size("node")
    local_count = lax.axis_size("local")
    owners = H // hidden_slice
    exp_group = local_count // owners
    experts = exp_group * node_count
    capacity = slot_rows // local_count
    expert_range = lax.iota(jnp.int32, experts)
    route_hits = expert_ids[:, :, None] == expert_range[None, None, :]
    dense_weights = jnp.sum(
        jnp.where(route_hits, route_weights[:, :, None].astype(jnp.float32), 0.0), axis=1
    ).astype(jnp.bfloat16)
    cohort_grad, cohort_weights = (
        lax.all_gather(grad_out, "node", axis=0, tiled=True),
        lax.all_gather(dense_weights, "node", axis=0, tiled=True),
    )
    group_index = lax.axis_index("node")
    group_weights = lax.dynamic_slice_in_dim(cohort_weights, group_index * exp_group, exp_group, 1)
    routed = (group_weights != 0).astype(jnp.int32)
    earlier = jnp.cumsum(routed, axis=0) - routed
    slot_range = lax.iota(jnp.int32, capacity)
    select = (routed[:, :, None] == 1) & (earlier[:, :, None] == slot_range[None, None, :])
    select_half = select.astype(jnp.bfloat16)
    packed = jnp.einsum(
        "cjs,cd->jsd", select_half, cohort_grad, preferred_element_type=jnp.float32
    ).astype(jnp.bfloat16)
    packed_weights = jnp.einsum(
        "cjs,cj->js", select_half, group_weights, preferred_element_type=jnp.float32
    ).astype(jnp.bfloat16)
    send_grad = jnp.broadcast_to(packed[:, None], (exp_group, owners, capacity, width)).reshape(
        local_count, capacity, width
    )
    send_weights = jnp.broadcast_to(packed_weights[:, None], (exp_group, owners, capacity)).reshape(
        local_count, capacity
    )
    recv_grad, recv_weights = (
        lax.all_to_all(send_grad, "local", split_axis=0, concat_axis=0, tiled=True),
        lax.all_to_all(send_weights, "local", split_axis=0, concat_axis=0, tiled=True),
    )
    cotangent = recv_grad.reshape(slot_rows, width)
    weight = recv_weights.reshape(slot_rows, 1).astype(jnp.float32)
    gate_value = gate_pre.astype(jnp.float32)
    up_value = up_pre.astype(jnp.float32)
    backward = jnp.dot(cotangent, w_down_t, preferred_element_type=jnp.float32)
    sigmoid_gate = jax.nn.sigmoid(gate_value)
    activated = gate_value * sigmoid_gate
    hidden = activated * up_value
    shares = jnp.sum(hidden * backward, axis=1).astype(jnp.bfloat16)
    scaled = weight * backward
    grad_gate_pre = (
        scaled * up_value * sigmoid_gate * (1.0 + gate_value * (1.0 - sigmoid_gate))
    ).astype(jnp.bfloat16)
    grad_up_pre = (scaled * activated).astype(jnp.bfloat16)
    weighted = (weight * hidden).astype(jnp.bfloat16)
    returned = lax.all_to_all(
        shares.reshape(local_count, capacity), "local", split_axis=0, concat_axis=0, tiled=True
    )
    slice_sum = jnp.sum(returned.astype(jnp.float32).reshape(exp_group, owners, capacity), axis=1)
    grad_route = jnp.sum(jnp.where(select, slice_sum[None], 0.0), axis=2).astype(jnp.bfloat16)
    half_width = width // lax.axis_size("rep")
    replica = lax.axis_index("rep")
    own_cols = lax.dynamic_slice_in_dim(cotangent, replica * half_width, half_width, 1)
    peer_cols = lax.dynamic_slice_in_dim(cotangent, (1 - replica) * half_width, half_width, 1)
    got_cols, got_weighted = swapped((peer_cols, weighted), "rep", 0)
    own_term = outer_term(own_cols, weighted).astype(jnp.bfloat16).astype(jnp.float32)
    peer_term = outer_term(got_cols, got_weighted).astype(jnp.bfloat16).astype(jnp.float32)
    grad_down_t = (own_term + peer_term).astype(jnp.bfloat16)
    return (grad_gate_pre, grad_up_pre, grad_down_t, grad_route)


def per_device(grad_out, expert_ids, route_weights, gate_pre, up_pre, w_down_t):
    nodes, locals_ = lax.axis_size("node"), lax.axis_size("local")
    capacity = gate_pre.shape[0] // locals_
    group_tok = grad_out.shape[0] * expert_ids.shape[1] // PER_GROUP
    args = (grad_out, expert_ids, route_weights, gate_pre, up_pre, w_down_t)
    if group_tok > capacity:
        return exchanged(*args)
    return gathered(nodes, locals_, group_tok, *args)


def solution(mesh):
    placed = (
        P(("node", "local", "rep"), None),
        P(("node", "local", "rep"), None),
        P(("node", "local", "rep"), None),
        P("rep", ("node", "local")),
        P("rep", ("node", "local")),
        P(None, ("node", "local")),
    )
    return jax.shard_map(
        per_device,
        mesh=mesh,
        in_specs=placed,
        out_specs=(
            P("rep", ("node", "local")),
            P("rep", ("node", "local")),
            P("rep", ("node", "local")),
            P(("local", "rep"), "node"),
        ),
        check_vma=False,
    )
```
